128 devices in a mesh: gz: 32 (over y, z_hi, x), xy: 4 (over z_lo, core).
Axes of the slice: x: 4, y: 4, z: 4 (z_hi: 2, z_lo: 2; z = z_hi * 2 + z_lo), core: 2. Of those that a mesh axis runs over, the one named last changes fastest.
Arguments:
- raw_volume: bfloat16 [64, 512, 512], P('gz', 'xy'), may hold values from -6 to 6
- weight_first: bfloat16 [32, 1, 3, 3], replicated, may hold values from -3 to 3
- bias_first: float32 [32], replicated, may hold values from -3 to 3
- weight_second: bfloat16 [64, 32, 3, 3], replicated, may hold values from -0.5 to 0.5
- bias_second: float32 [64], replicated, may hold values from -3 to 3
- weight_third: bfloat16 [128, 64, 3, 3], replicated, may hold values from -0.375 to 0.375
- bias_third: float32 [128], replicated, may hold values from -3 to 3
- weight_iso_a: bfloat16 [3, 3, 3, 128, 256], replicated, may hold values from -0.15625 to 0.15625
- bias_iso_a: float32 [256], replicated, may hold values from -3 to 3
- weight_iso_b: bfloat16 [3, 3, 3, 256, 256], replicated, may hold values from -0.109375 to 0.109375
- bias_iso_b: float32 [256], replicated, may hold values from -3 to 3
Outputs:
- features: bfloat16 [64, 64, 64, 256], P(None, 'xy', 'gz')
The draws below stay inside these ranges and needn't reach their ends.
All inputs are finite; a program needn't handle non-finite values.
Results may differ from the reference program's by a relative error of at most 0.0069.
Values may be sent and summed in bfloat16 or wider, within the bound.
A program may use at most 128 MiB of HBM per device.

```python
import jax
import jax.numpy as jnp
from jax import lax

H = 512
W = 512
C0 = 32
C1 = 64
C2 = 128
C3 = 256
Z = 64


def block_scale(stream_key, shape, shards, least, high):
    loudness = 1.0
    for position, blocks in shards:
        draws = jax.random.uniform(jax.random.fold_in(jax.random.fold_in(stream_key, 6), position), (blocks,), jnp.float32, least / len(shards), high / len(shards))
        loudness = loudness * jnp.repeat(jnp.exp(draws), shape[position] // blocks).reshape((-1,) + (1,) * (len(shape) - 1 - position))
    return loudness


def bell_draw(stream_key, dims, deviation, most, shards=(), held_as=jnp.bfloat16):
    values = deviation * jax.random.normal(stream_key, dims, jnp.float32)
    if shards:
        values = values * block_scale(stream_key, dims, shards, -0.22, 0.18)
    return jnp.clip(values, -most, most).astype(held_as)


def setup_inputs(seed: int = 0) -> dict:
    seeds = jax.random.split(jax.random.key(seed), 12)
    raw_volume = bell_draw(seeds[0], (Z, H, W), 1.0, 6.0, ((0, 32), (1, 4)))
    weight_first = bell_draw(seeds[1], (C0, 1, 3, 3), 4 ** -0.5, 3.0)
    bias_first = bell_draw(seeds[2], (C0,), 0.3, 3.0, (), jnp.float32)
    weight_second = bell_draw(seeds[3], (C1, C0, 3, 3), (9 * C0 // 2) ** -0.5, 0.5)
    bias_second = bell_draw(seeds[4], (C1,), 0.3, 3.0, (), jnp.float32)
    weight_third = bell_draw(seeds[5], (C2, C1, 3, 3), (9 * C1 // 2) ** -0.5, 0.375)
    bias_third = bell_draw(seeds[6], (C2,), 0.3, 3.0, (), jnp.float32)
    weight_iso_a = bell_draw(seeds[7], (3, 3, 3, C2, C3), (27 * C2 // 2) ** -0.5, 0.15625)
    bias_iso_a = bell_draw(seeds[8], (C3,), 0.3, 3.0, (), jnp.float32)
    weight_iso_b = bell_draw(seeds[9], (3, 3, 3, C3, C3), (27 * C3 // 2) ** -0.5, 0.109375)
    bias_iso_b = bell_draw(seeds[10], (C3,), 0.3, 3.0, (), jnp.float32)
    return {"raw_volume": raw_volume, "weight_first": weight_first, "bias_first": bias_first, "weight_second": weight_second, "bias_second": bias_second, "weight_third": weight_third, "bias_third": bias_third, "weight_iso_a": weight_iso_a, "bias_iso_a": bias_iso_a, "weight_iso_b": weight_iso_b, "bias_iso_b": bias_iso_b}


def pool_plane(values):
    sections, chans, height, breadth = values.shape
    return values.reshape(sections, chans, height // 2, 2, breadth // 2, 2).max(axis=(3, 5))


def plane_level(stack, weight, bias):
    def one_section(section):
        out = lax.conv_general_dilated(section[None].astype(jnp.float32), weight.astype(jnp.float32), (1, 1), ((1, 1), (1, 1)), dimension_numbers=("NCHW", "OIHW", "NCHW"), precision=lax.Precision.HIGHEST)
        out = out[0] + bias[:, None, None]
        return jnp.maximum(out, 0.0).astype(jnp.bfloat16)
    return pool_plane(lax.map(one_section, stack))


def cube_level(volume, weight, bias):
    out = lax.conv_general_dilated(volume[None].astype(jnp.float32), weight.astype(jnp.float32), (1, 1, 1), ((1, 1), (1, 1), (1, 1)), dimension_numbers=("NDHWC", "DHWIO", "NDHWC"), precision=lax.Precision.HIGHEST)
    return jnp.maximum(out[0] + bias, 0.0).astype(jnp.bfloat16)


def reference(raw_volume, weight_first, bias_first, weight_second, bias_second, weight_third, bias_third, weight_iso_a, bias_iso_a, weight_iso_b, bias_iso_b):
    stack = raw_volume[:, None, :, :]
    stack = plane_level(stack, weight_first, bias_first)
    stack = plane_level(stack, weight_second, bias_second)
    stack = plane_level(stack, weight_third, bias_third)
    volume = jnp.transpose(stack, (0, 2, 3, 1))
    middle = cube_level(volume, weight_iso_a, bias_iso_a)
    return cube_level(middle, weight_iso_b, bias_iso_b)
```

```python
import functools

import jax
import jax.numpy as jnp
from jax import lax
from jax.experimental import pallas as pl
from jax.experimental.pallas import tpu as pltpu
from jax.sharding import PartitionSpec as P

F32 = jnp.float32
BF16 = jnp.bfloat16
MESH = pl.DeviceIdType.MESH
VMEM = pl.BlockSpec(memory_space=pltpu.VMEM)
ANY = pl.BlockSpec(memory_space=pl.ANY)
ROWS = 168
WINS = 10


def picker():
    source = lax.broadcasted_iota(jnp.int32, (512, 1280), 0)
    column = lax.broadcasted_iota(jnp.int32, (512, 1280), 1)
    j, m = column // 128, column % 128
    x2 = 2 * (m % 64) + m // 64
    return (source == 4 * x2 - 3 + j).astype(BF16)


def banded_first(weight):
    taps = jnp.tile(jnp.transpose(weight[:, 0], (1, 2, 0)), (1, 1, 8))
    lane = lax.broadcasted_iota(jnp.int32, (10, 256), 1)
    j = lax.broadcasted_iota(jnp.int32, (10, 256), 0)
    first = 2 * ((lane // 32) % 4) + lane // 128
    rows = lax.broadcasted_iota(jnp.int32, (16, 10, 24, 256), 2)
    step = lax.broadcasted_iota(jnp.int32, (16, 10, 24, 256), 0)
    total = jnp.zeros((16, 10, 24, 256), BF16)
    for ky in range(3):
        cols = jnp.zeros((10, 256), BF16)
        for kx in range(3):
            cols = jnp.where(j == first + kx, taps[ky, kx][None, :], cols)
        total = jnp.where(rows == step + 1 + ky, cols[None, :, None, :], total)
    return jnp.pad(total.reshape(16, 240, 256), ((0, 0), (0, 16), (0, 0)))


def banded_second(weight):
    taps = jnp.transpose(weight, (2, 3, 1, 0))
    parts = [
        jnp.pad(taps, ((py, 1 - py), (px, 1 - px), (0, 0), (0, 0))).reshape(512, 64)
        for py in range(2)
        for px in range(2)
    ]
    return jnp.concatenate(parts, axis=1)


def banded_third(weight):
    taps = jnp.transpose(weight, (2, 3, 1, 0))
    parts = [jnp.pad(taps, ((0, 0), (px, 1 - px), (0, 0), (0, 0))).reshape(768, 128) for px in range(2)]
    return jnp.concatenate(parts, axis=1)


def plane_kernel(raw, pick, w1, b1, w2, b2, w3, b3, out, spread, turned, first, second, third):
    yi = lax.axis_index("xy")
    ny = lax.axis_size("xy")
    lane = lax.broadcasted_iota(jnp.int32, (128, 128), 1)
    sub = lax.broadcasted_iota(jnp.int32, (128, 128), 0)
    inside = jnp.logical_not(
        jnp.logical_or(
            jnp.logical_and(sub == 0, lane < 32), jnp.logical_and(sub == 127, lane >= 96)
        )
    )
    inside_f = jnp.where(inside, 1.0, 0.0)
    lane64 = lax.broadcasted_iota(jnp.int32, (64, 128), 1)
    sub64 = lax.broadcasted_iota(jnp.int32, (64, 128), 0)

    @pl.loop(0, 2)
    def _(z):
        spread[...] = jnp.dot(raw[z], pick[...], preferred_element_type=F32)

        @pl.loop(0, WINS)
        def _(w):
            rows = pl.ds(pl.multiple_of(w * 16, 16), 24)
            parts = [spread[rows, j * 128 : (j + 1) * 128] for j in range(10)]
            parts.append(jnp.zeros((16, 128), F32))
            turned[w] = jnp.concatenate(parts, axis=0).T.astype(BF16)

        @pl.loop(0, 8)
        def _(i):
            for w0 in range(0, WINS, 2):
                lhs = turned[w0 : w0 + 2].reshape(256, 256)
                one = jnp.dot(lhs, w1[2 * i], preferred_element_type=F32)
                two = jnp.dot(lhs, w1[2 * i + 1], preferred_element_type=F32)
                top = jnp.maximum(one, two)
                top = jnp.maximum(top[:, :128], top[:, 128:])
                top = jnp.maximum(top + b1[...], 0.0).reshape(2, 128, 128)
                for k in range(2):
                    row = 8 * (w0 + k) + i
                    place = 64 * yi + row - 7
                    valid = jnp.logical_and(place >= 0, place < 64 * ny)
                    scale = inside_f * jnp.where(valid, 1.0, 0.0)
                    first[row] = (top[k] * scale).astype(BF16)

        @pl.loop(0, 19)
        def _(g):
            base = 4 * g
            lhs = jnp.concatenate(
                [
                    jnp.concatenate([first[base + 2 * k + a] for a in range(4)], axis=1)
                    for k in range(2)
                ],
                axis=0,
            )
            res = jnp.dot(lhs, w2[...], preferred_element_type=F32)
            top = jnp.maximum(res[:, :128], res[:, 128:])
            top = jnp.maximum(top, pltpu.roll(top, 64, 1))
            top = jnp.maximum(top + b2[...], 0.0)
            for k in range(2):
                q = 2 * g + k
                place = 32 * yi + q - 3
                valid = jnp.logical_and(place >= 0, place < 32 * ny)
                val = top[128 * k : 128 * k + 128] * jnp.where(valid, 1.0, 0.0)
                even, odd = val[:64], val[64:]
                down = jnp.where(sub64 == 0, 0.0, pltpu.roll(odd, 1, 0))
                up = jnp.where(sub64 == 63, 0.0, pltpu.roll(even, 63, 0))
                second[q, :, :128] = jnp.where(lane64 < 64, down, even).astype(BF16)
                second[q, :, 128:] = jnp.where(lane64 < 64, odd, up).astype(BF16)

        @pl.loop(0, 9)
        def _(g):
            base = 4 * g
            lhs = jnp.concatenate(
                [second[pl.ds(base + ky, 4)].reshape(256, 256) for ky in range(3)], axis=1
            )
            res = jnp.dot(lhs, w3[...], preferred_element_type=F32)
            top = jnp.maximum(res[:, :128], res[:, 128:]).reshape(2, 2, 64, 128)
            top = jnp.maximum(top[:, 0], top[:, 1])
            top = jnp.maximum(top + b3[...], 0.0)
            for k in range(2):
                t = 2 * g + k
                place = 16 * yi + t - 1
                valid = jnp.logical_and(place >= 0, place < 16 * ny)
                third[t] = top[k] * jnp.where(valid, 1.0, 0.0)

        for t in range(18, 24):
            third[t] = jnp.zeros((64, 128), F32)
        out[0, z] = jnp.zeros((24, 128), BF16)
        out[65, z] = jnp.zeros((24, 128), BF16)

        @pl.loop(0, 8)
        def _(g):
            x0 = pl.multiple_of(8 * g, 8)
            block = third[:, pl.ds(x0, 8), :]
            out[pl.ds(1 + x0, 8), z] = jnp.transpose(block, (1, 0, 2)).astype(BF16)


def plane_levels(raw, pick, w1, b1, w2, b2, w3, b3):
    return pl.pallas_call(
        plane_kernel,
        name="plane_levels",
        out_shape=jax.ShapeDtypeStruct((66, 2, 24, 128), BF16),
        in_specs=[VMEM] * 8,
        out_specs=VMEM,
        scratch_shapes=[
            pltpu.VMEM((ROWS, 1280), F32),
            pltpu.VMEM((WINS, 128, 256), BF16),
            pltpu.VMEM((80, 128, 128), BF16),
            pltpu.VMEM((38, 64, 256), BF16),
            pltpu.VMEM((24, 64, 128), F32),
        ],
        compiler_params=pltpu.CompilerParams(vmem_limit_bytes=40 << 20),
    )(raw, pick, w1, b1, w2, b2, w3, b3)


def turn_kernel(peers, slab, brick, send_sem, recv_sem, local_sem):
    me = lax.axis_index("gz")
    yi = lax.axis_index("xy")

    barrier = pltpu.get_barrier_semaphore()

    @pl.loop(1, peers)
    def _(k):
        pl.semaphore_signal(
            barrier, inc=1, device_id=(lax.rem(me + k, peers), yi), device_id_type=MESH
        )

    pl.semaphore_wait(barrier, peers - 1)

    def copy(k):
        there = lax.rem(me + k, peers)
        return pltpu.make_async_remote_copy(
            src_ref=slab.at[pl.ds(2 * there, 4)],
            dst_ref=brick.at[:, pl.ds(2 * me, 2)],
            send_sem=send_sem.at[k],
            recv_sem=recv_sem.at[k],
            device_id=(there, yi),
            device_id_type=MESH,
        )

    own = pltpu.make_async_copy(
        slab.at[pl.ds(2 * me, 4)], brick.at[:, pl.ds(2 * me, 2)], local_sem
    )
    own.start()

    @pl.loop(1, peers)
    def _(k):
        copy(k).start()

    own.wait()

    @pl.loop(1, peers)
    def _(k):
        copy(k).wait()


def turn(slab, peers):
    return pl.pallas_call(
        functools.partial(turn_kernel, peers),
        name="turn",
        out_shape=jax.ShapeDtypeStruct((4, 2 * peers, 24, 128), BF16),
        in_specs=[VMEM],
        out_specs=VMEM,
        scratch_shapes=[
            pltpu.SemaphoreType.DMA((peers,)),
            pltpu.SemaphoreType.DMA((peers,)),
            pltpu.SemaphoreType.DMA,
        ],
        compiler_params=pltpu.CompilerParams(collective_id=0, has_side_effects=True),
    )(slab)


def cube_kernel(depth, chans, brick, weight, bias, out, tall):
    for ky in range(3):
        for x in range(4):
            tall[ky, x, 0] = jnp.zeros((16, chans), BF16)
            tall[ky, x, depth + 1] = jnp.zeros((16, chans), BF16)

    @pl.loop(0, depth)
    def _(z):
        for x in range(4):
            rows = brick[x, z].astype(F32)
            for ky in range(3):
                tall[ky, x, z + 1] = rows[ky : ky + 16].astype(BF16)

    step = 16
    for x in range(2):

        @pl.loop(0, depth // step)
        def _(g):
            z0 = g * step
            lhs = jnp.concatenate(
                [
                    tall[ky, x + kx, pl.ds(z0 + kz, step)].reshape(step * 16, chans)
                    for kz in range(3)
                    for ky in range(3)
                    for kx in range(3)
                ],
                axis=1,
            )
            res = jnp.dot(lhs, weight[...], preferred_element_type=F32)
            res = jnp.maximum(res + bias[...], 0.0).astype(BF16)
            out[x, pl.ds(z0, step)] = res.reshape(step, 16, 256)


def cube(brick, weight, bias):
    _, depth, _, chans = brick.shape
    return pl.pallas_call(
        functools.partial(cube_kernel, depth, chans),
        name="cube",
        out_shape=jax.ShapeDtypeStruct((2, depth, 16, 256), BF16),
        in_specs=[VMEM] * 3,
        out_specs=VMEM,
        scratch_shapes=[pltpu.VMEM((3, 4, depth + 2, 16, chans), BF16)],
        compiler_params=pltpu.CompilerParams(vmem_limit_bytes=56 << 20),
    )(brick, weight.reshape(27 * chans, 256), bias.reshape(1, 256))


def shift(block, axis, forward):
    count = lax.axis_size(axis)
    pairs = [(i, i + 1) for i in range(count - 1)]
    if not forward:
        pairs = [(b, a) for a, b in pairs]
    return lax.ppermute(block, axis, pairs)


def body(raw, wf, bf, ws, bs, wt, bt, wa, ba, wb, bb):
    low = shift(raw[:, 112:], "xy", True)
    high = shift(raw[:, :16], "xy", False)
    padded = jnp.concatenate([low, raw, high, jnp.zeros((2, 8, 512), BF16)], axis=1)
    slab = plane_levels(
        padded,
        picker(),
        banded_first(wf),
        jnp.tile(bf, 4).reshape(1, 128),
        banded_second(ws),
        jnp.tile(bs, 2).reshape(1, 128),
        banded_third(wt),
        bt.reshape(1, 128),
    )
    brick = turn(slab, lax.axis_size("gz"))
    middle = cube(brick, wa, ba)
    above = shift(middle[:, :, 15:], "xy", True)
    below = shift(middle[:, :, :1], "xy", False)
    middle = jnp.concatenate([above, middle, below, jnp.zeros((2, 64, 6, 256), BF16)], axis=2)
    left = shift(middle[1:], "gz", True)
    right = shift(middle[:1], "gz", False)
    out = cube(jnp.concatenate([left, middle, right], axis=0), wb, bb)
    return jnp.transpose(out, (1, 2, 0, 3))


def solution(mesh):
    placed = (P("gz", "xy", None), P(), P(), P(), P(), P(), P(), P(), P(), P(), P())
    return jax.shard_map(
        body, mesh=mesh, in_specs=placed, out_specs=P(None, "xy", "gz", None), check_vma=False
    )
```

```python
import functools

import jax
import jax.numpy as jnp
from jax import lax
from jax.experimental import pallas as pl
from jax.experimental.pallas import tpu as pltpu
from jax.sharding import PartitionSpec as P

F32 = jnp.float32
BF16 = jnp.bfloat16
MESH = pl.DeviceIdType.MESH
VMEM = pl.BlockSpec(memory_space=pltpu.VMEM)
ANY = pl.BlockSpec(memory_space=pl.ANY)
ROWS = 168
WINS = 10
CHUNKS = ((0, 4, 0, 7), (4, 7, 7, 13), (7, 10, 13, 19))


def picker():
    source = lax.broadcasted_iota(jnp.int32, (512, 1280), 0)
    column = lax.broadcasted_iota(jnp.int32, (512, 1280), 1)
    j, m = column // 128, column % 128
    x2 = 2 * (m % 64) + m // 64
    return (source == 4 * x2 - 3 + j).astype(BF16)


def banded_first(weight):
    taps = jnp.tile(jnp.transpose(weight[:, 0], (1, 2, 0)), (1, 1, 8))
    lane = lax.broadcasted_iota(jnp.int32, (10, 256), 1)
    j = lax.broadcasted_iota(jnp.int32, (10, 256), 0)
    first = 2 * ((lane // 32) % 4) + lane // 128
    rows = lax.broadcasted_iota(jnp.int32, (16, 10, 24, 256), 2)
    step = lax.broadcasted_iota(jnp.int32, (16, 10, 24, 256), 0)
    total = jnp.zeros((16, 10, 24, 256), BF16)
    for ky in range(3):
        cols = jnp.zeros((10, 256), BF16)
        for kx in range(3):
            cols = jnp.where(j == first + kx, taps[ky, kx][None, :], cols)
        total = jnp.where(rows == step + 1 + ky, cols[None, :, None, :], total)
    return jnp.pad(total.reshape(16, 240, 256), ((0, 0), (0, 16), (0, 0)))


def banded_second(weight):
    taps = jnp.transpose(weight, (2, 3, 1, 0))
    parts = [
        jnp.pad(taps, ((py, 1 - py), (px, 1 - px), (0, 0), (0, 0))).reshape(512, 64)
        for py in range(2)
        for px in range(2)
    ]
    return jnp.concatenate(parts, axis=1)


def banded_third(weight):
    taps = jnp.transpose(weight, (2, 3, 1, 0))
    parts = [jnp.pad(taps, ((0, 0), (px, 1 - px), (0, 0), (0, 0))).reshape(768, 128) for px in range(2)]
    return jnp.concatenate(parts, axis=1)


def shifted(rows):
    sub = lax.broadcasted_iota(jnp.int32, rows.shape, 0)
    last = rows.shape[0] - 1
    down = jnp.where(sub == 0, 0.0, pltpu.roll(rows, 1, 0))
    up = jnp.where(sub == last, 0.0, pltpu.roll(rows, last, 0))
    return down, up


def kernel(
    nx, ny, raw, pick, w1, b1, w2, b2, w3, b3, wa_hbm, ba, wb_hbm, bb,
    out,
    padded, spread, turned, first, second, third, slab, brick, tall, mid, wa, wb,
    raw_send, raw_recv, turn_send, turn_recv, own_sem, load_sem,
    side_send, side_recv, edge_send, edge_recv, corner_send, corner_recv,
):
    me = lax.axis_index("gz")
    yi = lax.axis_index("xy")
    has = {-1: yi > 0, 1: yi < ny - 1}
    hasx = {-1: me > 0, 1: me < nx - 1}

    load_a = pltpu.make_async_copy(wa_hbm, wa, load_sem.at[0])
    load_b = pltpu.make_async_copy(wb_hbm, wb, load_sem.at[1])
    load_a.start()
    load_b.start()

    barrier = pltpu.get_barrier_semaphore()

    def greet(gx, gy):
        pl.semaphore_signal(barrier, inc=1, device_id=(gx, gy), device_id_type=MESH)

    @pl.loop(1, nx)
    def _(k):
        greet(lax.rem(me + k, nx), yi)

    for dy in (-1, 1):

        @pl.when(has[dy])
        def _():
            greet(me, yi + dy)

        for dx in (-1, 1):

            @pl.when(jnp.logical_and(has[dy], hasx[dx]))
            def _():
                greet(me + dx, yi + dy)

    one = lambda flag: jnp.where(flag, 1, 0)
    tall_n = one(has[-1]) + one(has[1])
    wide_n = one(hasx[-1]) + one(hasx[1])
    pl.semaphore_wait(barrier, nx - 1 + tall_n + tall_n * wide_n)

    def raw_copy(dy):
        k = (dy + 1) // 2
        src = raw.at[:, pl.ds(112 if dy == 1 else 0, 16)]
        dst = padded.at[:, pl.ds(0 if dy == 1 else 144, 16)]
        return pltpu.make_async_remote_copy(
            src_ref=src, dst_ref=dst, send_sem=raw_send.at[k], recv_sem=raw_recv.at[k],
            device_id=(me, yi + dy), device_id_type=MESH,
        )

    for dy in (-1, 1):

        @pl.when(has[dy])
        def _():
            raw_copy(dy).start()

        @pl.when(jnp.logical_not(has[dy]))
        def _():
            padded[:, pl.ds(0 if dy == -1 else 144, 16)] = jnp.zeros((2, 16, 512), BF16)

    padded[:, pl.ds(16, 128)] = raw[...]
    padded[:, pl.ds(160, 8)] = jnp.zeros((2, 8, 512), BF16)
    for dx in (-1, 1):

        @pl.when(jnp.logical_not(hasx[dx]))
        def _():
            col = 0 if dx == -1 else 3

            @pl.loop(0, 18)
            def _(r):
                for kz in range(3):
                    mid[kz, col, r] = jnp.zeros((64, 256), BF16)

    for dy in (-1, 1):

        @pl.when(jnp.logical_not(has[dy]))
        def _():
            row = 0 if dy == -1 else 17
            for kz in range(3):
                for x in range(4):
                    mid[kz, x, row] = jnp.zeros((64, 256), BF16)

    for c in range(3):
        slab[c, 0] = jnp.zeros((2, 8, 128), BF16)
        slab[c, 65] = jnp.zeros((2, 8, 128), BF16)

    for dy in (-1, 1):

        @pl.when(has[dy])
        def _():
            raw_copy(dy).wait_send()

        @pl.when(has[-dy])
        def _():
            raw_copy(dy).wait_recv()

    lane = lax.broadcasted_iota(jnp.int32, (128, 128), 1)
    sub = lax.broadcasted_iota(jnp.int32, (128, 128), 0)
    outside = jnp.logical_or(
        jnp.logical_and(sub == 0, lane < 32), jnp.logical_and(sub == 127, lane >= 96)
    )
    inside_f = jnp.where(outside, 0.0, 1.0)
    lane64 = lax.broadcasted_iota(jnp.int32, (64, 128), 1)
    half = lane64 < 64

    def keep(place, size):
        return jnp.where(jnp.logical_and(place >= 0, place < size * ny), 1.0, 0.0)

    @pl.loop(0, 2)
    def _(z):
        spread[...] = jnp.dot(padded[z], pick[...], preferred_element_type=F32)

        @pl.loop(0, WINS)
        def _(w):
            rows = pl.ds(pl.multiple_of(w * 16, 16), 24)
            parts = [spread[rows, j * 128 : (j + 1) * 128] for j in range(10)]
            parts.append(jnp.zeros((16, 128), F32))
            turned[w, z] = jnp.concatenate(parts, axis=0).T.astype(BF16)

    def turn_copy(c, k):
        there = lax.rem(me + k, nx)
        return pltpu.make_async_remote_copy(
            src_ref=slab.at[c, pl.ds(2 * there, 4)],
            dst_ref=brick.at[c, :, pl.ds(2 * me, 2)],
            send_sem=turn_send.at[c, k],
            recv_sem=turn_recv.at[c, k],
            device_id=(there, yi),
            device_id_type=MESH,
        )

    def own_copy(c):
        return pltpu.make_async_copy(
            slab.at[c, pl.ds(2 * me, 4)], brick.at[c, :, pl.ds(2 * me, 2)], own_sem.at[c]
        )

    for c, (w_begin, w_end, p_begin, p_end) in enumerate(CHUNKS):

        @pl.loop(0, 8)
        def _(i):
            for w in range(w_begin, w_end):
                lhs = turned[w].reshape(256, 256)
                top = jnp.maximum(
                    jnp.dot(lhs, w1[2 * i], preferred_element_type=F32),
                    jnp.dot(lhs, w1[2 * i + 1], preferred_element_type=F32),
                )
                top = jnp.maximum(top[:, :128], top[:, 128:])
                top = jnp.maximum(top + b1[...], 0.0).reshape(2, 128, 128)
                row = 8 * w + i
                scale = inside_f * keep(64 * yi + row - 7, 64)
                for z in range(2):
                    first[z, row] = (top[z] * scale).astype(BF16)

        @pl.loop(p_begin, p_end)
        def _(g):
            base = 4 * g
            lhs = jnp.concatenate(
                [
                    jnp.concatenate([first[z, base + 2 * k + a] for a in range(4)], axis=1)
                    for z in range(2)
                    for k in range(2)
                ],
                axis=0,
            )
            res = jnp.dot(lhs, w2[...], preferred_element_type=F32)
            top = jnp.maximum(res[:, :128], res[:, 128:])
            top = jnp.maximum(top, pltpu.roll(top, 64, 1))
            top = jnp.maximum(top + b2[...], 0.0).reshape(2, 2, 128, 128)
            for k in range(2):
                q = 2 * g + k
                scale = keep(32 * yi + q - 3, 32)
                for z in range(2):
                    val = top[z, k] * scale
                    even, odd = val[:64], val[64:]
                    down = shifted(odd)[0]
                    up = shifted(even)[1]
                    second[z, q, :, :128] = jnp.where(half, down, even).astype(BF16)
                    second[z, q, :, 128:] = jnp.where(half, odd, up).astype(BF16)

        @pl.loop(3 * c, 3 * c + 3)
        def _(g):
            base = 4 * g
            lhs = jnp.concatenate(
                [
                    jnp.concatenate(
                        [second[z, pl.ds(base + ky, 4)].reshape(256, 256) for ky in range(3)], axis=1
                    )
                    for z in range(2)
                ],
                axis=0,
            )
            res = jnp.dot(lhs, w3[...], preferred_element_type=F32)
            top = jnp.maximum(res[:, :128], res[:, 128:]).reshape(2, 2, 2, 64, 128)
            top = jnp.maximum(top[:, :, 0], top[:, :, 1])
            top = jnp.maximum(top + b3[...], 0.0)
            for k in range(2):
                t = 2 * g + k
                scale = keep(16 * yi + t - 1, 16)
                for z in range(2):
                    third[z, t - 6 * c] = top[z, k] * scale

        for z in range(2):
            for r in range(6, 8):
                third[z, r] = jnp.zeros((64, 128), F32)

            @pl.loop(0, 8)
            def _(g):
                x0 = pl.multiple_of(8 * g, 8)
                block = third[z, :, pl.ds(x0, 8), :]
                slab[c, pl.ds(1 + x0, 8), z] = jnp.transpose(block, (1, 0, 2)).astype(BF16)

        own_copy(c).start()

        @pl.loop(1, nx)
        def _(k):
            turn_copy(c, k).start()

    def side_copy(dx, g):
        k = (dx + 1) // 2
        rows = pl.ds(1 + 2 * g, 2)
        return pltpu.make_async_remote_copy(
            src_ref=mid.at[1, 1 if dx == -1 else 2, rows],
            dst_ref=mid.at[1, 3 if dx == -1 else 0, rows],
            send_sem=side_send.at[k, g], recv_sem=side_recv.at[k, g],
            device_id=(me + dx, yi), device_id_type=MESH,
        )

    def edge_copy(dy):
        k = (dy + 1) // 2
        return pltpu.make_async_remote_copy(
            src_ref=mid.at[1, pl.ds(1, 2), 1 if dy == -1 else 16],
            dst_ref=mid.at[1, pl.ds(1, 2), 17 if dy == -1 else 0],
            send_sem=edge_send.at[k], recv_sem=edge_recv.at[k],
            device_id=(me, yi + dy), device_id_type=MESH,
        )

    def corner_copy(dx, dy):
        k, j = (dx + 1) // 2, (dy + 1) // 2
        return pltpu.make_async_remote_copy(
            src_ref=mid.at[1, 1 if dx == -1 else 2, 1 if dy == -1 else 16],
            dst_ref=mid.at[1, 3 if dx == -1 else 0, 17 if dy == -1 else 0],
            send_sem=corner_send.at[k, j], recv_sem=corner_recv.at[k, j],
            device_id=(me + dx, yi + dy), device_id_type=MESH,
        )

    def send_sides(g):
        for dx in (-1, 1):

            @pl.when(hasx[dx])
            def _():
                side_copy(dx, g).start()

    def send_edges(dy):
        @pl.when(has[dy])
        def _():
            edge_copy(dy).start()

        for dx in (-1, 1):

            @pl.when(jnp.logical_and(has[dy], hasx[dx]))
            def _():
                corner_copy(dx, dy).start()

    def cube_rows(source, weight, g, chans):
        lhs = jnp.concatenate(
            [
                jnp.concatenate(
                    [
                        source[kz, x + kx, pl.ds(2 * g + ky, 2)].reshape(128, chans)
                        for kz in range(3)
                        for ky in range(3)
                        for kx in range(3)
                    ],
                    axis=1,
                )
                for x in range(2)
            ],
            axis=0,
        )
        return jnp.dot(lhs, weight[...], preferred_element_type=F32)

    load_a.wait()
    for c, (g_begin, g_end) in enumerate(((0, 2), (2, 5), (5, 8))):
        own_copy(c).wait()

        @pl.loop(1, nx)
        def _(k):
            turn_copy(c, k).wait_recv()

        @pl.loop(0, 4)
        def _(x):
            rows = jnp.transpose(brick[c, x].astype(F32), (1, 0, 2))
            for r in range(6):
                down, up = shifted(rows[r])
                tall[0, x, 6 * c + r] = down.astype(BF16)
                tall[1, x, 6 * c + r] = rows[r].astype(BF16)
                tall[2, x, 6 * c + r] = up.astype(BF16)

        @pl.loop(g_begin, g_end)
        def _(g):
            res = cube_rows(tall, wa, g, 128)
            res = jnp.maximum(res + ba[...], 0.0).reshape(2, 2, 64, 256)
            for x in range(2):
                for r in range(2):
                    down, up = shifted(res[x, r])
                    mid[0, 1 + x, 1 + 2 * g + r] = down.astype(BF16)
                    mid[1, 1 + x, 1 + 2 * g + r] = res[x, r].astype(BF16)
                    mid[2, 1 + x, 1 + 2 * g + r] = up.astype(BF16)
            send_sides(g)

        if c == 0:
            send_edges(-1)
        if c == 2:
            send_edges(1)

    def spread_row(x, r):
        down, up = shifted(mid[1, x, r].astype(F32))
        mid[0, x, r] = down.astype(BF16)
        mid[2, x, r] = up.astype(BF16)

    def take_sides(g):
        for dx in (-1, 1):

            @pl.when(hasx[-dx])
            def _():
                side_copy(dx, g).wait_recv()
                for r in range(2):
                    spread_row(3 if dx == -1 else 0, 1 + 2 * g + r)

    def take_edges(dy):
        row = 17 if dy == -1 else 0

        @pl.when(has[-dy])
        def _():
            edge_copy(dy).wait_recv()
            spread_row(1, row)
            spread_row(2, row)

        for dx in (-1, 1):

            @pl.when(jnp.logical_and(has[-dy], hasx[-dx]))
            def _():
                corner_copy(dx, dy).wait_recv()
                spread_row(3 if dx == -1 else 0, row)

    def last_rows(g):
        res = cube_rows(mid, wb, g, 256)
        res = jnp.maximum(res + bb[...], 0.0).astype(BF16).reshape(2, 2, 64, 256)
        for x in range(2):
            for r in range(2):
                out[x, 2 * g + r] = res[x, r]

    load_b.wait()
    take_sides(0)
    take_sides(1)

    @pl.loop(1, 7)
    def _(g):
        take_sides(g + 1)
        last_rows(g)

    take_edges(-1)
    last_rows(7)
    take_edges(1)
    last_rows(0)

    for c in range(3):

        @pl.loop(1, nx)
        def _(k):
            turn_copy(c, k).wait_send()

    for dx in (-1, 1):

        @pl.when(hasx[dx])
        def _():
            @pl.loop(0, 8)
            def _(g):
                side_copy(dx, g).wait_send()

    for dy in (-1, 1):

        @pl.when(has[dy])
        def _():
            edge_copy(dy).wait_send()

        for dx in (-1, 1):

            @pl.when(jnp.logical_and(has[dy], hasx[dx]))
            def _():
                corner_copy(dx, dy).wait_send()


def body(raw, wf, bf, ws, bs, wt, bt, wa, ba, wb, bb):
    nx, ny = lax.axis_size("gz"), lax.axis_size("xy")
    dma = pltpu.SemaphoreType.DMA
    out = pl.pallas_call(
        functools.partial(kernel, nx, ny),
        name="encoder",
        out_shape=jax.ShapeDtypeStruct((2, 16, 64, 256), BF16),
        in_specs=[VMEM] * 8 + [ANY, VMEM, ANY, VMEM],
        out_specs=VMEM,
        scratch_shapes=[
            pltpu.VMEM((2, ROWS, 512), BF16),
            pltpu.VMEM((ROWS, 1280), F32),
            pltpu.VMEM((WINS, 2, 128, 256), BF16),
            pltpu.VMEM((2, 80, 128, 128), BF16),
            pltpu.VMEM((2, 38, 64, 256), BF16),
            pltpu.VMEM((2, 8, 64, 128), F32),
            pltpu.VMEM((3, 66, 2, 8, 128), BF16),
            pltpu.VMEM((3, 4, 64, 8, 128), BF16),
            pltpu.VMEM((3, 4, 18, 64, 128), BF16),
            pltpu.VMEM((3, 4, 18, 64, 256), BF16),
            pltpu.VMEM((27 * 128, 256), BF16),
            pltpu.VMEM((27 * 256, 256), BF16),
            dma((2,)), dma((2,)), dma((3, nx)), dma((3, nx)), dma((3,)), dma((2,)),
            dma((2, 8)), dma((2, 8)), dma((2,)), dma((2,)), dma((2, 2)), dma((2, 2)),
        ],
        compiler_params=pltpu.CompilerParams(
            collective_id=0, has_side_effects=True, vmem_limit_bytes=60 << 20
        ),
    )(
        raw,
        picker(),
        banded_first(wf),
        jnp.tile(bf, 4).reshape(1, 128),
        banded_second(ws),
        jnp.tile(bs, 2).reshape(1, 128),
        banded_third(wt),
        bt.reshape(1, 128),
        wa.reshape(27 * 128, 256),
        ba.reshape(1, 256),
        wb.reshape(27 * 256, 256),
        bb.reshape(1, 256),
    )
    return jnp.transpose(out, (2, 1, 0, 3))


def solution(mesh):
    placed = (P("gz", "xy", None), P(), P(), P(), P(), P(), P(), P(), P(), P(), P())
    return jax.shard_map(
        body, mesh=mesh, in_specs=placed, out_specs=P(None, "xy", "gz", None), check_vma=False
    )
```

```python
import functools

import jax
import jax.numpy as jnp
from jax import lax
from jax.experimental import pallas as pl
from jax.experimental.pallas import tpu as pltpu
from jax.sharding import PartitionSpec as P

F32 = jnp.float32
BF16 = jnp.bfloat16
MESH = pl.DeviceIdType.MESH
VMEM = pl.BlockSpec(memory_space=pltpu.VMEM)
ANY = pl.BlockSpec(memory_space=pl.ANY)
ROWS = 168
WINS = 5
CHUNKS = (((0, 2), (0, 14), (0, 6)), ((2, 4), (14, 30), (6, 14)), ((4, 5), (30, 38), (14, 18)))
TILE = (8, 8, 4)


def banded_second(weight):
    taps = jnp.transpose(weight, (2, 3, 1, 0))
    parts = [
        jnp.pad(taps, ((py, 1 - py), (px, 1 - px), (0, 0), (0, 0))).reshape(512, 64)
        for py in range(2)
        for px in range(2)
    ]
    return jnp.concatenate(parts, axis=1)


def banded_third(weight):
    taps = jnp.transpose(weight, (2, 3, 1, 0))
    parts = [jnp.pad(taps, ((0, 0), (px, 1 - px), (0, 0), (0, 0))).reshape(768, 128) for px in range(2)]
    return jnp.concatenate(parts, axis=1)


def shifted(rows):
    sub = lax.broadcasted_iota(jnp.int32, rows.shape, 0)
    last = rows.shape[0] - 1
    down = jnp.where(sub == 0, 0.0, pltpu.roll(rows, 1, 0))
    up = jnp.where(sub == last, 0.0, pltpu.roll(rows, last, 0))
    return down, up


def make_pick(pick):
    source = lax.broadcasted_iota(jnp.int32, (512, 128), 0)
    m = lax.broadcasted_iota(jnp.int32, (512, 128), 1)
    start = 8 * jnp.where(m < 64, m, m - 64) + jnp.where(m < 64, 0, 4) - 1
    gap = source - start
    for j in range(6):
        pick[:, 128 * j : 128 * j + 128] = jnp.where(gap == j, 1.0, 0.0).astype(BF16)


def make_first(small, w1):
    lane = lax.broadcasted_iota(jnp.int32, (1, 256), 1)
    bit = lambda n: jnp.where(jnp.bitwise_and(lane, n) == 0, 0, 1)
    start = 2 * (1 - bit(32)) + bit(64)
    cols = []
    for j in range(6):
        for ky in range(3):
            total = jnp.zeros((1, 256), F32)
            for kx in range(3):
                total = jnp.where(start == j - kx, small[3 * ky + kx : 3 * ky + kx + 1, :], total)
            cols.append(jnp.broadcast_to(total, (40, 256)))
    wide = lax.broadcasted_iota(jnp.int32, (40, 256), 1)
    gap = lax.broadcasted_iota(jnp.int32, (40, 256), 0) - jnp.where(wide < 128, 1, 2)

    @pl.loop(0, 16)
    def _(i):
        hit = [gap == 2 * i + ky for ky in range(3)]
        for j in range(6):
            total = jnp.zeros((40, 256), F32)
            for ky in range(3):
                total = jnp.where(hit[ky], cols[3 * j + ky], total)
            w1[i, 40 * j : 40 * j + 40] = total.astype(BF16)
        w1[i, 240:] = jnp.zeros((16, 256), BF16)


def kernel(
    nx, ny, raw, small, w2, w3, wa_hbm, wb_hbm,
    out,
    padded, pick, w1, spread, turned, first, second, third,
    slab_0, slab_1, slab_2, brick_0, brick_1, brick_2, tall, mid, wa, wb,
    raw_send, raw_recv, turn_send, turn_recv, own_sem, load_sem,
    side_send, side_recv, edge_send, edge_recv, corner_send, corner_recv,
):
    me = lax.axis_index("gz")
    yi = lax.axis_index("xy")
    slab, brick = (slab_0, slab_1, slab_2), (brick_0, brick_1, brick_2)
    has = {-1: yi > 0, 1: yi < ny - 1}
    hasx = {-1: me > 0, 1: me < nx - 1}

    load_a = pltpu.make_async_copy(wa_hbm, wa, load_sem.at[0])
    load_b = pltpu.make_async_copy(wb_hbm, wb, load_sem.at[1])
    load_a.start()
    load_b.start()

    barrier = pltpu.get_barrier_semaphore()

    def greet(gx, gy):
        pl.semaphore_signal(barrier, inc=1, device_id=(gx, gy), device_id_type=MESH)

    @pl.loop(1, nx)
    def _(k):
        greet(lax.rem(me + k, nx), yi)

    for dy in (-1, 1):

        @pl.when(has[dy])
        def _():
            greet(me, yi + dy)

        for dx in (-1, 1):

            @pl.when(jnp.logical_and(has[dy], hasx[dx]))
            def _():
                greet(me + dx, yi + dy)

    make_pick(pick)
    one = lambda flag: jnp.where(flag, 1, 0)
    tall_n = one(has[-1]) + one(has[1])
    wide_n = one(hasx[-1]) + one(hasx[1])
    pl.semaphore_wait(barrier, nx - 1 + tall_n + tall_n * wide_n)

    def raw_copy(dy):
        k = (dy + 1) // 2
        src = raw.at[:, pl.ds(112 if dy == 1 else 0, 16)]
        dst = padded.at[:, pl.ds(0 if dy == 1 else 144, 16)]
        return pltpu.make_async_remote_copy(
            src_ref=src, dst_ref=dst, send_sem=raw_send.at[k], recv_sem=raw_recv.at[k],
            device_id=(me, yi + dy), device_id_type=MESH,
        )

    for dy in (-1, 1):

        @pl.when(has[dy])
        def _():
            raw_copy(dy).start()

        @pl.when(jnp.logical_not(has[dy]))
        def _():
            padded[:, pl.ds(0 if dy == -1 else 144, 16)] = jnp.zeros((2, 16, 512), BF16)

    padded[:, pl.ds(16, 128)] = raw[...]
    padded[:, pl.ds(160, 8)] = jnp.zeros((2, 8, 512), BF16)
    for dx in (-1, 1):

        @pl.when(jnp.logical_not(hasx[dx]))
        def _():
            col = 0 if dx == -1 else 3

            @pl.loop(0, 18)
            def _(r):
                for kz in range(3):
                    mid[kz, col, r] = jnp.zeros((64, 256), BF16)

    for dy in (-1, 1):

        @pl.when(jnp.logical_not(has[dy]))
        def _():
            row = 0 if dy == -1 else 17
            for kz in range(3):
                for x in range(4):
                    mid[kz, x, row] = jnp.zeros((64, 256), BF16)

    for c in range(3):
        slab[c][0] = jnp.zeros((2, TILE[c], 128), BF16)
        slab[c][65] = jnp.zeros((2, TILE[c], 128), BF16)
    make_first(small, w1)

    for dy in (-1, 1):

        @pl.when(has[dy])
        def _():
            raw_copy(dy).wait_send()

        @pl.when(has[-dy])
        def _():
            raw_copy(dy).wait_recv()

    lane64 = lax.broadcasted_iota(jnp.int32, (64, 128), 1)
    low, high, half = lane64 < 32, lane64 >= 96, lane64 < 64
    b1, b2, b3 = small[9:10, :128], small[10:11, :128], small[11:12, :128]

    for z in range(2):
        spread[z] = jnp.dot(padded[z], pick[...], preferred_element_type=F32)
    for w in range(WINS):
        for z in range(2):
            parts = [spread[z, w * 32 : w * 32 + 40, j * 128 : (j + 1) * 128] for j in range(6)]
            parts.append(jnp.zeros((16, 128), F32))
            turned[w, z] = jnp.concatenate(parts, axis=0).T.astype(BF16)

    def turn_copy(c, k):
        there = lax.rem(me + k, nx)
        return pltpu.make_async_remote_copy(
            src_ref=slab[c].at[pl.ds(2 * there, 4)],
            dst_ref=brick[c].at[:, pl.ds(2 * me, 2)],
            send_sem=turn_send.at[c, k],
            recv_sem=turn_recv.at[c, k],
            device_id=(there, yi),
            device_id_type=MESH,
        )

    def own_copy(c):
        return pltpu.make_async_copy(
            slab[c].at[pl.ds(2 * me, 4)], brick[c].at[:, pl.ds(2 * me, 2)], own_sem.at[c]
        )

    def blank(ref, begin, end):
        for z in range(2):
            for r in range(begin, end):
                ref[z, r] = jnp.zeros(ref.shape[2:], ref.dtype)

    def outside(ref, c, above, below):
        if c == 0:
            pl.when(jnp.logical_not(has[-1]))(lambda: blank(ref, *above))
        if c == 2:
            pl.when(jnp.logical_not(has[1]))(lambda: blank(ref, *below))

    for c, ((w_begin, w_end), (q_begin, q_end), (t_begin, t_end)) in enumerate(CHUNKS):
        wins = w_end - w_begin
        for i in range(16):
            lhs = turned[w_begin:w_end].reshape(wins * 256, 256)
            res = jnp.dot(lhs, w1[i], preferred_element_type=F32)
            top = jnp.maximum(res[:, :128], res[:, 128:])
            top = jnp.maximum(top, pltpu.roll(top, 64, 1))
            top = jnp.maximum(top + b1, 0.0).reshape(wins, 2, 128, 128)
            for w in range(wins):
                for z in range(2):
                    even, odd = top[w, z, :64], top[w, z, 64:]
                    down, up = shifted(odd)[0], shifted(even)[1]
                    row = 16 * (w_begin + w) + i
                    left = jnp.where(low, down, jnp.where(high, odd, even))
                    right = jnp.where(low, even, jnp.where(high, up, odd))
                    first[z, row, :64] = left.astype(BF16)
                    first[z, row, 64:] = right.astype(BF16)
        outside(first, c, (0, 7), (71, 80))

        for q0 in range(q_begin, q_end, 2):
            lhs = jnp.concatenate(
                [
                    jnp.concatenate([first[z, 2 * (q0 + k) + a] for a in range(4)], axis=1)
                    for z in range(2)
                    for k in range(2)
                ],
                axis=0,
            )
            res = jnp.dot(lhs, w2[...], preferred_element_type=F32)
            top = jnp.maximum(res[:, :128], res[:, 128:])
            top = jnp.maximum(top, pltpu.roll(top, 64, 1))
            top = jnp.maximum(top + b2, 0.0).reshape(2, 2, 128, 128)
            for k in range(2):
                for z in range(2):
                    even, odd = top[z, k, :64], top[z, k, 64:]
                    down, up = shifted(odd)[0], shifted(even)[1]
                    second[z, q0 + k, :, :128] = jnp.where(half, down, even).astype(BF16)
                    second[z, q0 + k, :, 128:] = jnp.where(half, odd, up).astype(BF16)
        outside(second, c, (0, 3), (35, 38))

        nt = t_end - t_begin
        lhs = jnp.concatenate(
            [
                jnp.concatenate(
                    [
                        second[z, 2 * t_begin + ky : 2 * t_end + ky].reshape(nt * 128, 256)
                        for ky in range(3)
                    ],
                    axis=1,
                )
                for z in range(2)
            ],
            axis=0,
        )
        res = jnp.dot(lhs, w3[...], preferred_element_type=F32)
        top = jnp.maximum(res[:, :128], res[:, 128:]).reshape(2, nt, 2, 64, 128)
        top = jnp.maximum(top[:, :, 0], top[:, :, 1])
        top = jnp.maximum(top + b3, 0.0)
        for z in range(2):
            for r in range(nt):
                third[z, r] = top[z, r]
            for r in range(nt, TILE[c]):
                third[z, r] = jnp.zeros((64, 128), F32)
        outside(third, c, (0, 1), (nt - 1, nt))
        for z in range(2):
            for x0 in range(0, 64, 8):
                block = third[z, : TILE[c], x0 : x0 + 8, :]
                slab[c][1 + x0 : 9 + x0, z] = jnp.transpose(block, (1, 0, 2)).astype(BF16)

        own_copy(c).start()

        @pl.loop(1, nx)
        def _(k):
            turn_copy(c, k).start()

    def side_copy(dx, g):
        k = (dx + 1) // 2
        rows = pl.ds(1 + 4 * g, 4)
        return pltpu.make_async_remote_copy(
            src_ref=mid.at[1, 1 if dx == -1 else 2, rows],
            dst_ref=mid.at[1, 3 if dx == -1 else 0, rows],
            send_sem=side_send.at[k, g], recv_sem=side_recv.at[k, g],
            device_id=(me + dx, yi), device_id_type=MESH,
        )

    def edge_copy(dy):
        k = (dy + 1) // 2
        return pltpu.make_async_remote_copy(
            src_ref=mid.at[1, pl.ds(1, 2), 1 if dy == -1 else 16],
            dst_ref=mid.at[1, pl.ds(1, 2), 17 if dy == -1 else 0],
            send_sem=edge_send.at[k], recv_sem=edge_recv.at[k],
            device_id=(me, yi + dy), device_id_type=MESH,
        )

    def corner_copy(dx, dy):
        k, j = (dx + 1) // 2, (dy + 1) // 2
        return pltpu.make_async_remote_copy(
            src_ref=mid.at[1, 1 if dx == -1 else 2, 1 if dy == -1 else 16],
            dst_ref=mid.at[1, 3 if dx == -1 else 0, 17 if dy == -1 else 0],
            send_sem=corner_send.at[k, j], recv_sem=corner_recv.at[k, j],
            device_id=(me + dx, yi + dy), device_id_type=MESH,
        )

    def send_sides(g):
        for dx in (-1, 1):

            @pl.when(hasx[dx])
            def _():
                side_copy(dx, g).start()

    def send_edges(dy):
        @pl.when(has[dy])
        def _():
            edge_copy(dy).start()

        for dx in (-1, 1):

            @pl.when(jnp.logical_and(has[dy], hasx[dx]))
            def _():
                corner_copy(dx, dy).start()

    def cube_rows(source, weight, y, rows, chans):
        lhs = jnp.concatenate(
            [
                jnp.concatenate(
                    [
                        source[kz, x + kx, y + ky : y + ky + rows].reshape(64 * rows, chans)
                        for kz in range(3)
                        for ky in range(3)
                        for kx in range(3)
                    ],
                    axis=1,
                )
                for x in range(2)
            ],
            axis=0,
        )
        return jnp.dot(lhs, weight[...], preferred_element_type=F32)

    ba, bb = small[12:13, :], small[13:14, :]
    load_a.wait()
    for c, (y_begin, y_end) in enumerate(((0, 4), (4, 12), (12, 16))):
        t_begin, t_end = CHUNKS[c][2]
        own_copy(c).wait()

        @pl.loop(1, nx)
        def _(k):
            turn_copy(c, k).wait_recv()

        for x in range(4):
            rows = jnp.transpose(brick[c][x].astype(F32), (1, 0, 2))
            for r in range(t_end - t_begin):
                down, up = shifted(rows[r])
                tall[0, x, t_begin + r] = down.astype(BF16)
                tall[1, x, t_begin + r] = rows[r].astype(BF16)
                tall[2, x, t_begin + r] = up.astype(BF16)

        for y in range(y_begin, y_end, 4):
            res = cube_rows(tall, wa, y, 4, 128)
            res = jnp.maximum(res + ba, 0.0).reshape(2, 4, 64, 256)
            for x in range(2):
                for r in range(4):
                    down, up = shifted(res[x, r])
                    mid[0, 1 + x, 1 + y + r] = down.astype(BF16)
                    mid[1, 1 + x, 1 + y + r] = res[x, r].astype(BF16)
                    mid[2, 1 + x, 1 + y + r] = up.astype(BF16)
            send_sides(y // 4)

        if c == 0:
            send_edges(-1)
        if c == 2:
            send_edges(1)

    def spread_row(x, r):
        down, up = shifted(mid[1, x, r].astype(F32))
        mid[0, x, r] = down.astype(BF16)
        mid[2, x, r] = up.astype(BF16)

    def take_sides(g):
        for dx in (-1, 1):

            @pl.when(hasx[-dx])
            def _():
                side_copy(dx, g).wait_recv()
                for r in range(4):
                    spread_row(3 if dx == -1 else 0, 1 + 4 * g + r)

    def take_edges(dy):
        row = 17 if dy == -1 else 0

        @pl.when(has[-dy])
        def _():
            edge_copy(dy).wait_recv()
            spread_row(1, row)
            spread_row(2, row)

        for dx in (-1, 1):

            @pl.when(jnp.logical_and(has[-dy], hasx[-dx]))
            def _():
                corner_copy(dx, dy).wait_recv()
                spread_row(3 if dx == -1 else 0, row)

    def last_rows(y):
        res = cube_rows(mid, wb, y, 4, 256)
        res = jnp.maximum(res + bb, 0.0).astype(BF16).reshape(2, 4, 64, 256)
        for x in range(2):
            for r in range(4):
                out[x, y + r] = res[x, r]

    load_b.wait()
    take_sides(0)
    take_sides(1)
    take_sides(2)
    last_rows(4)
    take_sides(3)
    last_rows(8)
    take_edges(-1)
    last_rows(12)
    take_edges(1)
    last_rows(0)

    for c in range(3):

        @pl.loop(1, nx)
        def _(k):
            turn_copy(c, k).wait_send()

    for dx in (-1, 1):

        @pl.when(hasx[dx])
        def _():
            @pl.loop(0, 4)
            def _(g):
                side_copy(dx, g).wait_send()

    for dy in (-1, 1):

        @pl.when(has[dy])
        def _():
            edge_copy(dy).wait_send()

        for dx in (-1, 1):

            @pl.when(jnp.logical_and(has[dy], hasx[dx]))
            def _():
                corner_copy(dx, dy).wait_send()


def body(raw, wf, bf, ws, bs, wt, bt, wa, ba, wb, bb):
    nx, ny = lax.axis_size("gz"), lax.axis_size("xy")
    dma = pltpu.SemaphoreType.DMA
    taps = jnp.transpose(wf.reshape(32, 9)).astype(F32)
    small = jnp.concatenate(
        [
            jnp.tile(taps, (1, 8)),
            jnp.tile(bf, 8)[None],
            jnp.tile(bs, 4)[None],
            jnp.tile(bt, 2)[None],
            ba[None],
            bb[None],
            jnp.zeros((2, 256), F32),
        ],
        axis=0,
    )
    out = pl.pallas_call(
        functools.partial(kernel, nx, ny),
        name="encoder",
        out_shape=jax.ShapeDtypeStruct((2, 16, 64, 256), BF16),
        in_specs=[VMEM] * 4 + [ANY, ANY],
        out_specs=VMEM,
        scratch_shapes=[
            pltpu.VMEM((2, ROWS, 512), BF16),
            pltpu.VMEM((512, 768), BF16),
            pltpu.VMEM((16, 256, 256), BF16),
            pltpu.VMEM((2, ROWS, 768), F32),
            pltpu.VMEM((WINS, 2, 128, 256), BF16),
            pltpu.VMEM((2, 80, 128, 128), BF16),
            pltpu.VMEM((2, 38, 64, 256), BF16),
            pltpu.VMEM((2, 8, 64, 128), F32),
        ]
        + [pltpu.VMEM((66, 2, rows, 128), BF16) for rows in TILE]
        + [pltpu.VMEM((4, 64, rows, 128), BF16) for rows in TILE]
        + [
            pltpu.VMEM((3, 4, 18, 64, 128), BF16),
            pltpu.VMEM((3, 4, 18, 64, 256), BF16),
            pltpu.VMEM((27 * 128, 256), BF16),
            pltpu.VMEM((27 * 256, 256), BF16),
            dma((2,)), dma((2,)), dma((3, nx)), dma((3, nx)), dma((3,)), dma((2,)),
            dma((2, 4)), dma((2, 4)), dma((2,)), dma((2,)), dma((2, 2)), dma((2, 2)),
        ],
        compiler_params=pltpu.CompilerParams(
            collective_id=0, has_side_effects=True, vmem_limit_bytes=60 << 20
        ),
    )(
        raw,
        small,
        banded_second(ws),
        banded_third(wt),
        wa.reshape(27 * 128, 256),
        wb.reshape(27 * 256, 256),
    )
    return jnp.transpose(out, (2, 1, 0, 3))


def solution(mesh):
    placed = (P("gz", "xy", None), P(), P(), P(), P(), P(), P(), P(), P(), P(), P())
    return jax.shard_map(
        body, mesh=mesh, in_specs=placed, out_specs=P(None, "xy", "gz", None), check_vma=False
    )
```

```python
import functools

import jax
import jax.numpy as jnp
from jax import lax
from jax.experimental import pallas as pl
from jax.experimental.pallas import tpu as pltpu
from jax.sharding import PartitionSpec as P

F32 = jnp.float32
BF16 = jnp.bfloat16
MESH = pl.DeviceIdType.MESH
VMEM = pl.BlockSpec(memory_space=pltpu.VMEM)
ANY = pl.BlockSpec(memory_space=pl.ANY)
ROWS = 168
WINS = (1, 2, 3, 0, 4)
CHUNKS = (((12, 30), (6, 14), 8), ((0, 12), (0, 6), 8), ((30, 38), (14, 18), 4))
GROUPS = ((0, 6, 3), (0, 9, 3), (1, 3, 3), (1, 0, 3), (2, 12, 4))


def shifted(rows):
    sub = lax.broadcasted_iota(jnp.int32, rows.shape, 0)
    last = rows.shape[0] - 1
    down = jnp.where(sub == 0, 0.0, pltpu.roll(rows, 1, 0))
    up = jnp.where(sub == last, 0.0, pltpu.roll(rows, last, 0))
    return down, up


def make_pick(pick):
    source = lax.broadcasted_iota(jnp.int32, (512, 128), 0)
    m = lax.broadcasted_iota(jnp.int32, (512, 128), 1)
    start = 8 * jnp.where(m < 64, m, m - 64) + jnp.where(m < 64, 0, 4) - 1
    gap = source - start
    for j in range(6):
        pick[:, 128 * j : 128 * j + 128] = jnp.where(gap == j, 1.0, 0.0).astype(BF16)


def make_small(wf, small):
    for ky in range(3):
        for kx in range(3):
            row = wf[ky, kx : kx + 1, :].astype(F32)
            small[3 * ky + kx : 3 * ky + kx + 1, :] = jnp.concatenate([row] * 8, axis=1)


def make_first(small, w1):
    lane = lax.broadcasted_iota(jnp.int32, (1, 256), 1)
    bit = lambda n: jnp.where(jnp.bitwise_and(lane, n) == 0, 0, 1)
    start = 2 * (1 - bit(32)) + bit(64)
    cols = []
    for j in range(6):
        for ky in range(3):
            total = jnp.zeros((1, 256), F32)
            for kx in range(3):
                total = jnp.where(start == j - kx, small[3 * ky + kx : 3 * ky + kx + 1, :], total)
            cols.append(jnp.broadcast_to(total, (40, 256)))
    wide = lax.broadcasted_iota(jnp.int32, (40, 256), 1)
    gap = lax.broadcasted_iota(jnp.int32, (40, 256), 0) - jnp.where(wide < 128, 1, 2)

    @pl.loop(0, 16)
    def _(i):
        hit = [gap == 2 * i + ky for ky in range(3)]
        for j in range(6):
            total = jnp.zeros((40, 256), F32)
            for ky in range(3):
                total = jnp.where(hit[ky], cols[3 * j + ky], total)
            w1[i, 40 * j : 40 * j + 40] = total.astype(BF16)
        w1[i, 240:] = jnp.zeros((16, 256), BF16)


def make_second(ws, w2):
    w2[...] = jnp.zeros((512, 256), BF16)
    for py in range(2):
        for px in range(2):
            lanes = slice(64 * (2 * py + px), 64 * (2 * py + px) + 64)
            for ky in range(3):
                for kx in range(3):
                    row = 32 * (4 * (ky + py) + kx + px)
                    w2[row : row + 32, lanes] = ws[ky, kx]


def make_third(wt, w3):
    w3[...] = jnp.zeros((768, 256), BF16)
    for px in range(2):
        for ky in range(3):
            for kx in range(3):
                row = 256 * ky + 64 * (kx + px)
                w3[row : row + 64, 128 * px : 128 * px + 128] = wt[ky, kx]


def kernel(
    nx, ny, raw, wf, bf, ws, bs, wt, bt, wa_hbm, ba, wb_hbm, bb,
    out,
    above, below, small, pick, w1, w2, w3, spread, turned, first, second, third,
    slab_0, slab_1, slab_2, brick_0, brick_1, brick_2, tall, mid, wa, wb,
    raw_send, raw_recv, turn_send, turn_recv, own_sem, load_sem,
    side_send, side_recv, edge_send, edge_recv, corner_send, corner_recv,
):
    me = lax.axis_index("gz")
    yi = lax.axis_index("xy")
    slab, brick = (slab_0, slab_1, slab_2), (brick_0, brick_1, brick_2)
    has = {-1: yi > 0, 1: yi < ny - 1}
    hasx = {-1: me > 0, 1: me < nx - 1}

    load_a = pltpu.make_async_copy(wa_hbm, wa, load_sem.at[0])
    load_b = pltpu.make_async_copy(wb_hbm, wb, load_sem.at[1])
    load_a.start()
    load_b.start()

    barrier = pltpu.get_barrier_semaphore()

    def greet(gx, gy):
        pl.semaphore_signal(barrier, inc=1, device_id=(gx, gy), device_id_type=MESH)

    @pl.loop(1, nx)
    def _(k):
        greet(lax.rem(me + k, nx), yi)

    for dy in (-1, 1):

        @pl.when(has[dy])
        def _():
            greet(me, yi + dy)

        for dx in (-1, 1):

            @pl.when(jnp.logical_and(has[dy], hasx[dx]))
            def _():
                greet(me + dx, yi + dy)

    make_small(wf, small)
    make_pick(pick)
    make_first(small, w1)
    make_second(ws, w2)
    make_third(wt, w3)
    for z in range(2):
        spread[z, 16:144] = jnp.dot(raw[z], pick[...], preferred_element_type=F32)

    one = lambda flag: jnp.where(flag, 1, 0)
    tall_n = one(has[-1]) + one(has[1])
    wide_n = one(hasx[-1]) + one(hasx[1])
    pl.semaphore_wait(barrier, nx - 1 + tall_n + tall_n * wide_n)

    def raw_copy(dy):
        k = (dy + 1) // 2
        return pltpu.make_async_remote_copy(
            src_ref=raw.at[:, pl.ds(112 if dy == 1 else 0, 16)],
            dst_ref=above if dy == 1 else below,
            send_sem=raw_send.at[k], recv_sem=raw_recv.at[k],
            device_id=(me, yi + dy), device_id_type=MESH,
        )

    for dy in (-1, 1):

        @pl.when(has[dy])
        def _():
            raw_copy(dy).start()

        @pl.when(jnp.logical_not(has[dy]))
        def _():
            (above if dy == -1 else below)[...] = jnp.zeros((2, 16, 512), BF16)

    for dx in (-1, 1):

        @pl.when(jnp.logical_not(hasx[dx]))
        def _():
            col = 0 if dx == -1 else 3

            @pl.loop(0, 18)
            def _(r):
                for kz in range(3):
                    mid[kz, col, r] = jnp.zeros((64, 256), BF16)

    for dy in (-1, 1):

        @pl.when(jnp.logical_not(has[dy]))
        def _():
            row = 0 if dy == -1 else 17
            for kz in range(3):
                for x in range(4):
                    mid[kz, x, row] = jnp.zeros((64, 256), BF16)

    for c in range(3):
        slab[c][0] = jnp.zeros((2, CHUNKS[c][2], 128), BF16)
        slab[c][65] = jnp.zeros((2, CHUNKS[c][2], 128), BF16)

    lane64 = lax.broadcasted_iota(jnp.int32, (64, 128), 1)
    low, high, half = lane64 < 32, lane64 >= 96, lane64 < 64
    b1 = jnp.concatenate([bf[...]] * 4, axis=1)
    b2 = jnp.concatenate([bs[...]] * 2, axis=1)
    b3 = bt[...]

    def sent(c):
        (t_begin, t_end), stored = CHUNKS[c][1:]
        return pl.ds(0, t_end - t_begin)

    def turn_copy(c, k):
        there = lax.rem(me + k, nx)
        return pltpu.make_async_remote_copy(
            src_ref=slab[c].at[pl.ds(2 * there, 4), :, sent(c)],
            dst_ref=brick[c].at[:, pl.ds(2 * me, 2), sent(c)],
            send_sem=turn_send.at[c, k],
            recv_sem=turn_recv.at[c, k],
            device_id=(there, yi),
            device_id_type=MESH,
        )

    def own_copy(c):
        return pltpu.make_async_copy(
            slab[c].at[pl.ds(2 * me, 4), :, sent(c)],
            brick[c].at[:, pl.ds(2 * me, 2), sent(c)],
            own_sem.at[c],
        )

    def blank(ref, begin, end):
        for z in range(2):
            for r in range(begin, end):
                ref[z, r] = jnp.zeros(ref.shape[2:], ref.dtype)

    def blank_low(ref, begin, end):
        pl.when(jnp.logical_not(has[-1]))(lambda: blank(ref, begin, end))

    def blank_high(ref, begin, end):
        pl.when(jnp.logical_not(has[1]))(lambda: blank(ref, begin, end))

    def first_level(begin, end):
        wins = end - begin
        for n in range(begin, end):
            for z in range(2):
                rows = slice(WINS[n] * 32, WINS[n] * 32 + 40)
                parts = [spread[z, rows, j * 128 : (j + 1) * 128] for j in range(6)]
                parts.append(jnp.zeros((16, 128), F32))
                turned[n, z] = jnp.concatenate(parts, axis=0).T.astype(BF16)
        for i in range(16):
            lhs = turned[begin:end].reshape(wins * 256, 256)
            res = jnp.dot(lhs, w1[i], preferred_element_type=F32)
            top = jnp.maximum(res[:, :128], res[:, 128:])
            top = jnp.maximum(top, pltpu.roll(top, 64, 1))
            top = jnp.maximum(top + b1, 0.0).reshape(wins, 2, 128, 128)
            for w in range(wins):
                for z in range(2):
                    even, odd = top[w, z, :64], top[w, z, 64:]
                    down, up = shifted(odd)[0], shifted(even)[1]
                    row = 16 * WINS[begin + w] + i
                    left = jnp.where(low, down, jnp.where(high, odd, even))
                    right = jnp.where(low, even, jnp.where(high, up, odd))
                    first[z, row, :64] = left.astype(BF16)
                    first[z, row, 64:] = right.astype(BF16)

    def second_level(begin, end):
        for q0 in range(begin, end, 2):
            lhs = jnp.concatenate(
                [
                    jnp.concatenate([first[z, 2 * (q0 + k) + a] for a in range(4)], axis=1)
                    for z in range(2)
                    for k in range(2)
                ],
                axis=0,
            )
            res = jnp.dot(lhs, w2[...], preferred_element_type=F32)
            top = jnp.maximum(res[:, :128], res[:, 128:])
            top = jnp.maximum(top, pltpu.roll(top, 64, 1))
            top = jnp.maximum(top + b2, 0.0).reshape(2, 2, 128, 128)
            for k in range(2):
                for z in range(2):
                    even, odd = top[z, k, :64], top[z, k, 64:]
                    down, up = shifted(odd)[0], shifted(even)[1]
                    second[z, q0 + k, :, :128] = jnp.where(half, down, even).astype(BF16)
                    second[z, q0 + k, :, 128:] = jnp.where(half, odd, up).astype(BF16)

    def third_level(begin, end):
        nt = end - begin
        lhs = jnp.concatenate(
            [
                jnp.concatenate(
                    [
                        second[z, 2 * begin + ky : 2 * end + ky].reshape(nt * 128, 256)
                        for ky in range(3)
                    ],
                    axis=1,
                )
                for z in range(2)
            ],
            axis=0,
        )
        res = jnp.dot(lhs, w3[...], preferred_element_type=F32)
        top = jnp.maximum(res[:, :128], res[:, 128:]).reshape(2, nt, 2, 64, 128)
        top = jnp.maximum(top[:, :, 0], top[:, :, 1])
        top = jnp.maximum(top + b3, 0.0)
        for z in range(2):
            for r in range(nt):
                third[z, r] = top[z, r]

    def send(c):
        for z in range(2):
            for x0 in range(0, 64, 8):
                block = third[z, : CHUNKS[c][2], x0 : x0 + 8, :]
                slab[c][1 + x0 : 9 + x0, z] = jnp.transpose(block, (1, 0, 2)).astype(BF16)
        own_copy(c).start()

        @pl.loop(1, nx)
        def _(k):
            turn_copy(c, k).start()

    first_level(0, 3)
    second_level(*CHUNKS[0][0])
    third_level(*CHUNKS[0][1])
    send(0)

    for dy in (-1, 1):

        @pl.when(has[dy])
        def _():
            raw_copy(dy).wait_send()

        @pl.when(has[-dy])
        def _():
            raw_copy(dy).wait_recv()

    for z in range(2):
        rows = jnp.concatenate([above[z], below[z], jnp.zeros((16, 512), BF16)], axis=0)
        res = jnp.dot(rows, pick[...], preferred_element_type=F32)
        spread[z, :16] = res[:16]
        spread[z, 144:168] = res[16:40]
    first_level(3, 5)
    blank_low(first, 0, 7)
    blank_high(first, 71, 80)
    second_level(*CHUNKS[1][0])
    blank_low(second, 0, 3)
    third_level(*CHUNKS[1][1])
    blank_low(third, 0, 1)
    send(1)
    second_level(*CHUNKS[2][0])
    blank_high(second, 35, 38)
    third_level(*CHUNKS[2][1])
    blank_high(third, 3, 4)
    send(2)

    def side_copy(dx, g):
        k = (dx + 1) // 2
        rows = pl.ds(1 + GROUPS[g][1], GROUPS[g][2])
        return pltpu.make_async_remote_copy(
            src_ref=mid.at[1, 1 if dx == -1 else 2, rows],
            dst_ref=mid.at[1, 3 if dx == -1 else 0, rows],
            send_sem=side_send.at[k, g], recv_sem=side_recv.at[k, g],
            device_id=(me + dx, yi), device_id_type=MESH,
        )

    def edge_copy(dy):
        k = (dy + 1) // 2
        return pltpu.make_async_remote_copy(
            src_ref=mid.at[1, pl.ds(1, 2), 1 if dy == -1 else 16],
            dst_ref=mid.at[1, pl.ds(1, 2), 17 if dy == -1 else 0],
            send_sem=edge_send.at[k], recv_sem=edge_recv.at[k],
            device_id=(me, yi + dy), device_id_type=MESH,
        )

    def corner_copy(dx, dy):
        k, j = (dx + 1) // 2, (dy + 1) // 2
        return pltpu.make_async_remote_copy(
            src_ref=mid.at[1, 1 if dx == -1 else 2, 1 if dy == -1 else 16],
            dst_ref=mid.at[1, 3 if dx == -1 else 0, 17 if dy == -1 else 0],
            send_sem=corner_send.at[k, j], recv_sem=corner_recv.at[k, j],
            device_id=(me + dx, yi + dy), device_id_type=MESH,
        )

    def send_sides(g):
        for dx in (-1, 1):

            @pl.when(hasx[dx])
            def _():
                side_copy(dx, g).start()

    def send_edges(dy):
        @pl.when(has[dy])
        def _():
            edge_copy(dy).start()

        for dx in (-1, 1):

            @pl.when(jnp.logical_and(has[dy], hasx[dx]))
            def _():
                corner_copy(dx, dy).start()

    def cube_rows(source, weight, runs, chans):
        lhs = jnp.concatenate(
            [
                jnp.concatenate(
                    [
                        source[kz, x + kx, y + ky : y + ky + rows].reshape(64 * rows, chans)
                        for kz in range(3)
                        for ky in range(3)
                        for kx in range(3)
                    ],
                    axis=1,
                )
                for x in range(2)
                for y, rows in runs
            ],
            axis=0,
        )
        return jnp.dot(lhs, weight[...], preferred_element_type=F32)

    load_a.wait()
    arrived = -1
    for g, (c, y, rows) in enumerate(GROUPS):
        if c != arrived:
            arrived = c
            own_copy(c).wait()

            @pl.loop(1, nx)
            def _(k):
                turn_copy(c, k).wait_recv()

            t_begin, t_end = CHUNKS[c][1]
            for x in range(4):
                lines = jnp.transpose(brick[c][x].astype(F32), (1, 0, 2))
                for r in range(t_end - t_begin):
                    down, up = shifted(lines[r])
                    tall[0, x, t_begin + r] = down.astype(BF16)
                    tall[1, x, t_begin + r] = lines[r].astype(BF16)
                    tall[2, x, t_begin + r] = up.astype(BF16)

        res = cube_rows(tall, wa, ((y, rows),), 128)
        res = jnp.maximum(res + ba[...], 0.0).reshape(2, rows, 64, 256)
        for x in range(2):
            for r in range(rows):
                down, up = shifted(res[x, r])
                mid[0, 1 + x, 1 + y + r] = down.astype(BF16)
                mid[1, 1 + x, 1 + y + r] = res[x, r].astype(BF16)
                mid[2, 1 + x, 1 + y + r] = up.astype(BF16)
        if y == 0:
            send_edges(-1)
        if y == 12:
            send_edges(1)
        send_sides(g)

    def spread_row(x, r):
        down, up = shifted(mid[1, x, r].astype(F32))
        mid[0, x, r] = down.astype(BF16)
        mid[2, x, r] = up.astype(BF16)

    def take_sides(g):
        for dx in (-1, 1):

            @pl.when(hasx[-dx])
            def _():
                side_copy(dx, g).wait_recv()
                for r in range(GROUPS[g][2]):
                    spread_row(3 if dx == -1 else 0, 1 + GROUPS[g][1] + r)

    def take_edges(dy):
        row = 17 if dy == -1 else 0

        @pl.when(has[-dy])
        def _():
            edge_copy(dy).wait_recv()
            spread_row(1, row)
            spread_row(2, row)

        for dx in (-1, 1):

            @pl.when(jnp.logical_and(has[-dy], hasx[-dx]))
            def _():
                corner_copy(dx, dy).wait_recv()
                spread_row(3 if dx == -1 else 0, row)

    def last_rows(*runs):
        res = cube_rows(mid, wb, runs, 256)
        res = jnp.maximum(res + bb[...], 0.0).reshape(2, -1, 64, 256)
        lines = [y + r for y, rows in runs for r in range(rows)]
        for x in range(2):
            for r, line in enumerate(lines):
                out[:, line, x] = res[x, r].astype(BF16)

    load_b.wait()
    take_sides(0)
    take_sides(1)
    last_rows((7, 4))
    take_sides(2)
    last_rows((4, 3))
    take_sides(3)
    last_rows((1, 3))
    take_sides(4)
    last_rows((11, 4))
    take_edges(-1)
    take_edges(1)
    last_rows((0, 1), (15, 1))

    for c in range(3):

        @pl.loop(1, nx)
        def _(k):
            turn_copy(c, k).wait_send()

    for dx in (-1, 1):

        @pl.when(hasx[dx])
        def _():
            for g in range(5):
                side_copy(dx, g).wait_send()

    for dy in (-1, 1):

        @pl.when(has[dy])
        def _():
            edge_copy(dy).wait_send()

        for dx in (-1, 1):

            @pl.when(jnp.logical_and(has[dy], hasx[dx]))
            def _():
                corner_copy(dx, dy).wait_send()


def body(raw, wf, bf, ws, bs, wt, bt, wa, ba, wb, bb):
    nx, ny = lax.axis_size("gz"), lax.axis_size("xy")
    dma = pltpu.SemaphoreType.DMA
    return pl.pallas_call(
        functools.partial(kernel, nx, ny),
        name="encoder",
        out_shape=jax.ShapeDtypeStruct((64, 16, 2, 256), BF16),
        in_specs=[VMEM] * 7 + [ANY, VMEM, ANY, VMEM],
        out_specs=VMEM,
        scratch_shapes=[
            pltpu.VMEM((2, 16, 512), BF16),
            pltpu.VMEM((2, 16, 512), BF16),
            pltpu.VMEM((16, 256), F32),
            pltpu.VMEM((512, 768), BF16),
            pltpu.VMEM((16, 256, 256), BF16),
            pltpu.VMEM((512, 256), BF16),
            pltpu.VMEM((768, 256), BF16),
            pltpu.VMEM((2, ROWS, 768), F32),
            pltpu.VMEM((len(WINS), 2, 128, 256), BF16),
            pltpu.VMEM((2, 80, 128, 128), BF16),
            pltpu.VMEM((2, 38, 64, 256), BF16),
            pltpu.VMEM((2, 8, 64, 128), F32),
        ]
        + [pltpu.VMEM((66, 2, stored, 128), BF16) for _, _, stored in CHUNKS]
        + [pltpu.VMEM((4, 64, stored, 128), BF16) for _, _, stored in CHUNKS]
        + [
            pltpu.VMEM((3, 4, 18, 64, 128), BF16),
            pltpu.VMEM((3, 4, 18, 64, 256), BF16),
            pltpu.VMEM((27 * 128, 256), BF16),
            pltpu.VMEM((27 * 256, 256), BF16),
            dma((2,)), dma((2,)), dma((3, nx)), dma((3, nx)), dma((3,)), dma((2,)),
            dma((2, 5)), dma((2, 5)), dma((2,)), dma((2,)), dma((2, 2)), dma((2, 2)),
        ],
        compiler_params=pltpu.CompilerParams(
            collective_id=0, has_side_effects=True, vmem_limit_bytes=60 << 20
        ),
    )(
        raw,
        jnp.transpose(wf[:, 0], (1, 2, 0)),
        bf.reshape(1, 32),
        jnp.transpose(ws, (2, 3, 1, 0)),
        bs.reshape(1, 64),
        jnp.transpose(wt, (2, 3, 1, 0)),
        bt.reshape(1, 128),
        wa.reshape(27 * 128, 256),
        ba.reshape(1, 256),
        wb.reshape(27 * 256, 256),
        bb.reshape(1, 256),
    )


def solution(mesh):
    placed = (P("gz", "xy", None), P(), P(), P(), P(), P(), P(), P(), P(), P(), P())
    return jax.shard_map(
        body, mesh=mesh, in_specs=placed, out_specs=P(None, "xy", "gz", None), check_vma=False
    )
```

```python
import functools

import jax
import jax.numpy as jnp
from jax import lax
from jax.experimental import pallas as pl
from jax.experimental.pallas import tpu as pltpu
from jax.sharding import PartitionSpec as P

F32 = jnp.float32
BF16 = jnp.bfloat16
MESH = pl.DeviceIdType.MESH
VMEM = pl.BlockSpec(memory_space=pltpu.VMEM)
ANY = pl.BlockSpec(memory_space=pl.ANY)
ROWS = 168
WINS = (1, 2, 3, 0, 4)
CHUNKS = (((12, 30), (6, 14), 8), ((0, 12), (0, 6), 8), ((30, 38), (14, 18), 4))
GROUPS = ((0, 6, 3), (0, 9, 3), (1, 3, 3), (1, 0, 3), (2, 12, 4))


def shifted(rows):
    sub = lax.broadcasted_iota(jnp.int32, rows.shape, 0)
    last = rows.shape[0] - 1
    down = jnp.where(sub == 0, 0.0, pltpu.roll(rows, 1, 0))
    up = jnp.where(sub == last, 0.0, pltpu.roll(rows, last, 0))
    return down, up


def make_pick(pick):
    source = lax.broadcasted_iota(jnp.int32, (512, 128), 0)
    m = lax.broadcasted_iota(jnp.int32, (512, 128), 1)
    start = 8 * jnp.where(m < 64, m, m - 64) + jnp.where(m < 64, 0, 4) - 1
    gap = source - start
    for j in range(6):
        pick[:, 128 * j : 128 * j + 128] = jnp.where(gap == j, 1.0, 0.0).astype(BF16)


def make_small(wf, small):
    for ky in range(3):
        for kx in range(3):
            row = wf[ky, kx : kx + 1, :].astype(F32)
            small[3 * ky + kx : 3 * ky + kx + 1, :] = jnp.concatenate([row] * 8, axis=1)


def make_first(small, w1):
    lane = lax.broadcasted_iota(jnp.int32, (1, 256), 1)
    bit = lambda n: jnp.where(jnp.bitwise_and(lane, n) == 0, 0, 1)
    start = 2 * (1 - bit(32)) + bit(64)
    cols = []
    for j in range(6):
        for ky in range(3):
            total = jnp.zeros((1, 256), F32)
            for kx in range(3):
                total = jnp.where(start == j - kx, small[3 * ky + kx : 3 * ky + kx + 1, :], total)
            cols.append(jnp.broadcast_to(total, (40, 256)))
    wide = lax.broadcasted_iota(jnp.int32, (40, 256), 1)
    gap = lax.broadcasted_iota(jnp.int32, (40, 256), 0) - jnp.where(wide < 128, 1, 2)

    @pl.loop(0, 16)
    def _(i):
        hit = [gap == 2 * i + ky for ky in range(3)]
        for j in range(6):
            total = jnp.zeros((40, 256), F32)
            for ky in range(3):
                total = jnp.where(hit[ky], cols[3 * j + ky], total)
            w1[i, 40 * j : 40 * j + 40] = total.astype(BF16)
        w1[i, 240:] = jnp.zeros((16, 256), BF16)


def make_second(ws, w2):
    w2[...] = jnp.zeros((512, 256), BF16)
    for py in range(2):
        for px in range(2):
            lanes = slice(64 * (2 * py + px), 64 * (2 * py + px) + 64)
            for ky in range(3):
                for kx in range(3):
                    row = 32 * (4 * (ky + py) + kx + px)
                    w2[row : row + 32, lanes] = ws[ky, kx]


def make_third(wt, w3):
    w3[...] = jnp.zeros((768, 256), BF16)
    for px in range(2):
        for ky in range(3):
            for kx in range(3):
                row = 256 * ky + 64 * (kx + px)
                w3[row : row + 64, 128 * px : 128 * px + 128] = wt[ky, kx]


def kernel(
    nx, ny, raw, wf, bf, ws, bs, wt, bt, wa_hbm, ba, wb_hbm, bb,
    out,
    above, below, small, pick, w1, w2, w3, spread, turned, first, second, third,
    slab_0, slab_1, slab_2, brick_0, brick_1, brick_2, tall, mid, wa, wb,
    raw_send, raw_recv, turn_send, turn_recv, own_sem, load_sem,
    side_send, side_recv, edge_send, edge_recv, corner_send, corner_recv,
):
    me = lax.axis_index("gz")
    yi = lax.axis_index("xy")
    slab, brick = (slab_0, slab_1, slab_2), (brick_0, brick_1, brick_2)
    has = {-1: yi > 0, 1: yi < ny - 1}
    hasx = {-1: me > 0, 1: me < nx - 1}

    load_a = pltpu.make_async_copy(wa_hbm, wa, load_sem.at[0])
    load_b = pltpu.make_async_copy(wb_hbm, wb, load_sem.at[1])
    load_a.start()
    load_b.start()

    barrier = pltpu.get_barrier_semaphore()

    def greet(gx, gy):
        pl.semaphore_signal(barrier, inc=1, device_id=(gx, gy), device_id_type=MESH)

    @pl.loop(1, nx)
    def _(k):
        greet(lax.rem(me + k, nx), yi)

    for dy in (-1, 1):

        @pl.when(has[dy])
        def _():
            greet(me, yi + dy)

        for dx in (-1, 1):

            @pl.when(jnp.logical_and(has[dy], hasx[dx]))
            def _():
                greet(me + dx, yi + dy)

    make_small(wf, small)
    make_pick(pick)
    make_first(small, w1)
    make_second(ws, w2)
    make_third(wt, w3)
    for z in range(2):
        spread[z, 16:144] = jnp.dot(raw[z], pick[...], preferred_element_type=F32)

    one = lambda flag: jnp.where(flag, 1, 0)
    tall_n = one(has[-1]) + one(has[1])
    wide_n = one(hasx[-1]) + one(hasx[1])
    pl.semaphore_wait(barrier, nx - 1 + tall_n + tall_n * wide_n)

    def raw_copy(dy):
        k = (dy + 1) // 2
        return pltpu.make_async_remote_copy(
            src_ref=raw.at[:, pl.ds(112 if dy == 1 else 0, 16)],
            dst_ref=above if dy == 1 else below,
            send_sem=raw_send.at[k], recv_sem=raw_recv.at[k],
            device_id=(me, yi + dy), device_id_type=MESH,
        )

    for dy in (-1, 1):

        @pl.when(has[dy])
        def _():
            raw_copy(dy).start()

        @pl.when(jnp.logical_not(has[dy]))
        def _():
            (above if dy == -1 else below)[...] = jnp.zeros((2, 16, 512), BF16)

    for dx in (-1, 1):

        @pl.when(jnp.logical_not(hasx[dx]))
        def _():
            col = 0 if dx == -1 else 3

            @pl.loop(0, 18)
            def _(r):
                mid[1, col, r] = jnp.zeros((64, 256), BF16)

    for dy in (-1, 1):

        @pl.when(jnp.logical_not(has[dy]))
        def _():
            row = 0 if dy == -1 else 17
            for x in range(4):
                mid[1, x, row] = jnp.zeros((64, 256), BF16)

    for c in range(3):
        slab[c][0] = jnp.zeros((2, CHUNKS[c][2], 128), BF16)
        slab[c][65] = jnp.zeros((2, CHUNKS[c][2], 128), BF16)

    lane64 = lax.broadcasted_iota(jnp.int32, (64, 128), 1)
    low, high, half = lane64 < 32, lane64 >= 96, lane64 < 64
    b1 = jnp.concatenate([bf[...]] * 4, axis=1)
    b2 = jnp.concatenate([bs[...]] * 2, axis=1)
    b3 = bt[...]

    def sent(c):
        (t_begin, t_end), stored = CHUNKS[c][1:]
        return pl.ds(0, t_end - t_begin)

    def turn_copy(c, k):
        there = lax.rem(me + k, nx)
        return pltpu.make_async_remote_copy(
            src_ref=slab[c].at[pl.ds(2 * there, 4), :, sent(c)],
            dst_ref=brick[c].at[:, pl.ds(2 * me, 2), sent(c)],
            send_sem=turn_send.at[c, k],
            recv_sem=turn_recv.at[c, k],
            device_id=(there, yi),
            device_id_type=MESH,
        )

    def own_copy(c):
        return pltpu.make_async_copy(
            slab[c].at[pl.ds(2 * me, 4), :, sent(c)],
            brick[c].at[:, pl.ds(2 * me, 2), sent(c)],
            own_sem.at[c],
        )

    def blank(ref, begin, end):
        for z in range(2):
            for r in range(begin, end):
                ref[z, r] = jnp.zeros(ref.shape[2:], ref.dtype)

    def blank_low(ref, begin, end):
        pl.when(jnp.logical_not(has[-1]))(lambda: blank(ref, begin, end))

    def blank_high(ref, begin, end):
        pl.when(jnp.logical_not(has[1]))(lambda: blank(ref, begin, end))

    def first_level(begin, end):
        wins = end - begin
        for n in range(begin, end):
            for z in range(2):
                rows = slice(WINS[n] * 32, WINS[n] * 32 + 40)
                parts = [spread[z, rows, j * 128 : (j + 1) * 128] for j in range(6)]
                parts.append(jnp.zeros((16, 128), F32))
                turned[n, z] = jnp.concatenate(parts, axis=0).T.astype(BF16)
        for i in range(16):
            lhs = turned[begin:end].reshape(wins * 256, 256)
            res = jnp.dot(lhs, w1[i], preferred_element_type=F32)
            top = jnp.maximum(res[:, :128], res[:, 128:])
            top = jnp.maximum(top, pltpu.roll(top, 64, 1))
            top = jnp.maximum(top + b1, 0.0).reshape(wins, 2, 128, 128)
            for w in range(wins):
                for z in range(2):
                    even, odd = top[w, z, :64], top[w, z, 64:]
                    down, up = shifted(odd)[0], shifted(even)[1]
                    row = 16 * WINS[begin + w] + i
                    left = jnp.where(low, down, jnp.where(high, odd, even))
                    right = jnp.where(low, even, jnp.where(high, up, odd))
                    first[z, row, :64] = left.astype(BF16)
                    first[z, row, 64:] = right.astype(BF16)

    def second_level(begin, end):
        for q0 in range(begin, end, 2):
            lhs = jnp.concatenate(
                [
                    jnp.concatenate([first[z, 2 * (q0 + k) + a] for a in range(4)], axis=1)
                    for z in range(2)
                    for k in range(2)
                ],
                axis=0,
            )
            res = jnp.dot(lhs, w2[...], preferred_element_type=F32)
            top = jnp.maximum(res[:, :128], res[:, 128:])
            top = jnp.maximum(top, pltpu.roll(top, 64, 1))
            top = jnp.maximum(top + b2, 0.0).reshape(2, 2, 128, 128)
            for k in range(2):
                for z in range(2):
                    even, odd = top[z, k, :64], top[z, k, 64:]
                    down, up = shifted(odd)[0], shifted(even)[1]
                    second[z, q0 + k, :, :128] = jnp.where(half, down, even).astype(BF16)
                    second[z, q0 + k, :, 128:] = jnp.where(half, odd, up).astype(BF16)

    def third_level(begin, end):
        nt = end - begin
        lhs = jnp.concatenate(
            [
                jnp.concatenate(
                    [
                        second[z, 2 * begin + ky : 2 * end + ky].reshape(nt * 128, 256)
                        for ky in range(3)
                    ],
                    axis=1,
                )
                for z in range(2)
            ],
            axis=0,
        )
        res = jnp.dot(lhs, w3[...], preferred_element_type=F32)
        top = jnp.maximum(res[:, :128], res[:, 128:]).reshape(2, nt, 2, 64, 128)
        top = jnp.maximum(top[:, :, 0], top[:, :, 1])
        top = jnp.maximum(top + b3, 0.0)
        for z in range(2):
            for r in range(nt):
                third[z, r] = top[z, r]

    def send(c):
        for z in range(2):
            for x0 in range(0, 64, 8):
                block = third[z, : CHUNKS[c][2], x0 : x0 + 8, :]
                slab[c][1 + x0 : 9 + x0, z] = jnp.transpose(block, (1, 0, 2)).astype(BF16)
        own_copy(c).start()

        @pl.loop(1, nx)
        def _(k):
            turn_copy(c, k).start()

    first_level(0, 3)
    second_level(*CHUNKS[0][0])
    third_level(*CHUNKS[0][1])
    send(0)

    for dy in (-1, 1):

        @pl.when(has[dy])
        def _():
            raw_copy(dy).wait_send()

        @pl.when(has[-dy])
        def _():
            raw_copy(dy).wait_recv()

    for z in range(2):
        rows = jnp.concatenate([above[z], below[z], jnp.zeros((16, 512), BF16)], axis=0)
        res = jnp.dot(rows, pick[...], preferred_element_type=F32)
        spread[z, :16] = res[:16]
        spread[z, 144:168] = res[16:40]
    first_level(3, 5)
    blank_low(first, 0, 7)
    blank_high(first, 71, 80)
    second_level(*CHUNKS[1][0])
    blank_low(second, 0, 3)
    third_level(*CHUNKS[1][1])
    blank_low(third, 0, 1)
    send(1)
    second_level(*CHUNKS[2][0])
    blank_high(second, 35, 38)
    third_level(*CHUNKS[2][1])
    blank_high(third, 3, 4)
    send(2)

    def side_copy(dx, g):
        k = (dx + 1) // 2
        rows = pl.ds(1 + GROUPS[g][1], GROUPS[g][2])
        return pltpu.make_async_remote_copy(
            src_ref=mid.at[1, 1 if dx == -1 else 2, rows],
            dst_ref=mid.at[1, 3 if dx == -1 else 0, rows],
            send_sem=side_send.at[k, g], recv_sem=side_recv.at[k, g],
            device_id=(me + dx, yi), device_id_type=MESH,
        )

    def edge_copy(dy):
        k = (dy + 1) // 2
        return pltpu.make_async_remote_copy(
            src_ref=mid.at[1, pl.ds(1, 2), 1 if dy == -1 else 16],
            dst_ref=mid.at[1, pl.ds(1, 2), 17 if dy == -1 else 0],
            send_sem=edge_send.at[k], recv_sem=edge_recv.at[k],
            device_id=(me, yi + dy), device_id_type=MESH,
        )

    def corner_copy(dx, dy):
        k, j = (dx + 1) // 2, (dy + 1) // 2
        return pltpu.make_async_remote_copy(
            src_ref=mid.at[1, 1 if dx == -1 else 2, 1 if dy == -1 else 16],
            dst_ref=mid.at[1, 3 if dx == -1 else 0, 17 if dy == -1 else 0],
            send_sem=corner_send.at[k, j], recv_sem=corner_recv.at[k, j],
            device_id=(me + dx, yi + dy), device_id_type=MESH,
        )

    def send_sides(g):
        for dx in (-1, 1):

            @pl.when(hasx[dx])
            def _():
                side_copy(dx, g).start()

    def send_edges(dy):
        @pl.when(has[dy])
        def _():
            edge_copy(dy).start()

        for dx in (-1, 1):

            @pl.when(jnp.logical_and(has[dy], hasx[dx]))
            def _():
                corner_copy(dx, dy).start()

    def cube_rows(source, weight, runs, chans):
        lhs = jnp.concatenate(
            [
                jnp.concatenate(
                    [
                        source[kz, x + kx, y + ky : y + ky + rows].reshape(64 * rows, chans)
                        for kz in range(3)
                        for ky in range(3)
                        for kx in range(3)
                    ],
                    axis=1,
                )
                for x in range(2)
                for y, rows in runs
            ],
            axis=0,
        )
        return jnp.dot(lhs, weight[...], preferred_element_type=F32)

    load_a.wait()
    arrived = -1
    for g, (c, y, rows) in enumerate(GROUPS):
        if c != arrived:
            arrived = c
            own_copy(c).wait()

            @pl.loop(1, nx)
            def _(k):
                turn_copy(c, k).wait_recv()

            t_begin, t_end = CHUNKS[c][1]
            for x in range(4):
                lines = jnp.transpose(brick[c][x].astype(F32), (1, 0, 2))
                for r in range(t_end - t_begin):
                    down, up = shifted(lines[r])
                    tall[0, x, t_begin + r] = down.astype(BF16)
                    tall[1, x, t_begin + r] = lines[r].astype(BF16)
                    tall[2, x, t_begin + r] = up.astype(BF16)

        res = cube_rows(tall, wa, ((y, rows),), 128)
        res = jnp.maximum(res + ba[...], 0.0).reshape(2, rows, 64, 256)
        for x in range(2):
            for r in range(rows):
                down, up = shifted(res[x, r])
                mid[0, 1 + x, 1 + y + r] = down.astype(BF16)
                mid[1, 1 + x, 1 + y + r] = res[x, r].astype(BF16)
                mid[2, 1 + x, 1 + y + r] = up.astype(BF16)
        if y == 0:
            send_edges(-1)
        if y == 12:
            send_edges(1)
        send_sides(g)

    def spread_row(x, r):
        down, up = shifted(mid[1, x, r].astype(F32))
        mid[0, x, r] = down.astype(BF16)
        mid[2, x, r] = up.astype(BF16)

    def take_sides(*groups):
        for g in groups:
            for dx in (-1, 1):

                @pl.when(hasx[-dx])
                def _():
                    side_copy(dx, g).wait_recv()

        for g in groups:
            for r in range(GROUPS[g][2]):
                spread_row(0, 1 + GROUPS[g][1] + r)
                spread_row(3, 1 + GROUPS[g][1] + r)

    def take_edges():
        for dy in (-1, 1):

            @pl.when(has[-dy])
            def _():
                edge_copy(dy).wait_recv()

            for dx in (-1, 1):

                @pl.when(jnp.logical_and(has[-dy], hasx[-dx]))
                def _():
                    corner_copy(dx, dy).wait_recv()

        for x in range(4):
            spread_row(x, 0)
            spread_row(x, 17)

    def last_rows(*runs):
        res = cube_rows(mid, wb, runs, 256)
        res = jnp.maximum(res + bb[...], 0.0).reshape(2, -1, 64, 256)
        lines = [y + r for y, rows in runs for r in range(rows)]
        for x in range(2):
            for r, line in enumerate(lines):
                out[:, line, x] = res[x, r].astype(BF16)

    load_b.wait()
    take_sides(0, 1)
    last_rows((7, 4))
    take_sides(2)
    last_rows((4, 3))
    take_sides(3)
    last_rows((1, 3))
    take_sides(4)
    last_rows((11, 4))
    take_edges()
    last_rows((0, 1), (15, 1))

    for c in range(3):

        @pl.loop(1, nx)
        def _(k):
            turn_copy(c, k).wait_send()

    for dx in (-1, 1):

        @pl.when(hasx[dx])
        def _():
            for g in range(5):
                side_copy(dx, g).wait_send()

    for dy in (-1, 1):

        @pl.when(has[dy])
        def _():
            edge_copy(dy).wait_send()

        for dx in (-1, 1):

            @pl.when(jnp.logical_and(has[dy], hasx[dx]))
            def _():
                corner_copy(dx, dy).wait_send()


def hand_over(source, out, held, take, give):
    parts = take.shape[0]
    size = source.shape[0] // parts
    piece = lambda ref, p: ref.at[pl.ds(p * size, size)]
    loads = [pltpu.make_async_copy(piece(source, p), piece(held, p), take.at[p]) for p in range(parts)]
    stores = [pltpu.make_async_copy(piece(held, p), piece(out, p), give.at[p]) for p in range(parts)]
    for load in loads:
        load.start()
    for load, store in zip(loads, stores):
        load.wait()
        store.start()
    for store in stores:
        store.wait()


def body(raw, wf, bf, ws, bs, wt, bt, wa, ba, wb, bb):
    nx, ny = lax.axis_size("gz"), lax.axis_size("xy")
    dma = pltpu.SemaphoreType.DMA
    out = pl.pallas_call(
        functools.partial(kernel, nx, ny),
        name="encoder",
        out_shape=jax.ShapeDtypeStruct((64, 16, 2, 256), BF16),
        in_specs=[VMEM] * 7 + [ANY, VMEM, ANY, VMEM],
        out_specs=VMEM,
        scratch_shapes=[
            pltpu.VMEM((2, 16, 512), BF16),
            pltpu.VMEM((2, 16, 512), BF16),
            pltpu.VMEM((16, 256), F32),
            pltpu.VMEM((512, 768), BF16),
            pltpu.VMEM((16, 256, 256), BF16),
            pltpu.VMEM((512, 256), BF16),
            pltpu.VMEM((768, 256), BF16),
            pltpu.VMEM((2, ROWS, 768), F32),
            pltpu.VMEM((len(WINS), 2, 128, 256), BF16),
            pltpu.VMEM((2, 80, 128, 128), BF16),
            pltpu.VMEM((2, 38, 64, 256), BF16),
            pltpu.VMEM((2, 8, 64, 128), F32),
        ]
        + [pltpu.VMEM((66, 2, stored, 128), BF16) for _, _, stored in CHUNKS]
        + [pltpu.VMEM((4, 64, stored, 128), BF16) for _, _, stored in CHUNKS]
        + [
            pltpu.VMEM((3, 4, 18, 64, 128), BF16),
            pltpu.VMEM((3, 4, 18, 64, 256), BF16),
            pltpu.VMEM((27 * 128, 256), BF16),
            pltpu.VMEM((27 * 256, 256), BF16),
            dma((2,)), dma((2,)), dma((3, nx)), dma((3, nx)), dma((3,)), dma((2,)),
            dma((2, 5)), dma((2, 5)), dma((2,)), dma((2,)), dma((2, 2)), dma((2, 2)),
        ],
        compiler_params=pltpu.CompilerParams(
            collective_id=0, has_side_effects=True, vmem_limit_bytes=60 << 20
        ),
    )(
        raw,
        jnp.transpose(wf[:, 0], (1, 2, 0)),
        bf.reshape(1, 32),
        jnp.transpose(ws, (2, 3, 1, 0)),
        bs.reshape(1, 64),
        jnp.transpose(wt, (2, 3, 1, 0)),
        bt.reshape(1, 128),
        wa.reshape(27 * 128, 256),
        ba.reshape(1, 256),
        wb.reshape(27 * 256, 256),
        bb.reshape(1, 256),
    )
    return pl.pallas_call(
        hand_over,
        name="hand_over",
        out_shape=jax.ShapeDtypeStruct(out.shape, BF16),
        in_specs=[ANY],
        out_specs=ANY,
        scratch_shapes=[pltpu.VMEM(out.shape, BF16), dma((4,)), dma((4,))],
        compiler_params=pltpu.CompilerParams(vmem_limit_bytes=60 << 20),
    )(out)


def solution(mesh):
    placed = (P("gz", "xy", None), P(), P(), P(), P(), P(), P(), P(), P(), P(), P())
    return jax.shard_map(
        body, mesh=mesh, in_specs=placed, out_specs=P(None, "xy", "gz", None), check_vma=False
    )
```
